512 devices in a mesh: gx: 8 (over y, core), gy: 8 (over z_lo), gz: 8 (over x, z_hi).
Axes of the slice: x: 4, y: 4, z: 16 (z_hi: 2, z_lo: 8; z = z_hi * 8 + z_lo), core: 2. Of those that a mesh axis runs over, the one named last changes fastest.
Arguments:
- charges: float32 [8, 128, 128, 1024], P(None, 'gx', 'gy', 'gz'), may hold values from -120 to 120
- permittivity: float32 [128, 128, 1024], P('gx', 'gy', 'gz'), may hold values from 1 to 8
- screening: float32 [128, 128, 1024], P('gx', 'gy', 'gz'), may hold values from 0.05 to 2
Outputs:
- top_power: float32 [8, 128, 128, 1024], P(None, 'gx', 'gy', 'gz')
- r_factor: float32 [40, 40], replicated
The draws below stay inside these ranges and needn't reach their ends.
All inputs are finite; a program needn't handle non-finite values.
Results may differ from the reference program's by a relative error of at most 0.0002.
Values sent between devices are 32-bit elements; how exact they have to be, the bound alone decides.
A program may use at most 64 MiB of HBM per device.

```python
import math
import jax
import jax.numpy as jnp
from jax import lax

NRHS = 8
BASIS = 4
NX = 128
NY = 128
NZ = 1024


def draw_charges(key, part):
    key_base, key_rough = jax.random.split(key, 2)
    full_shape = (NRHS, NX, NY, NZ)
    base = jnp.clip(jax.random.normal(key_base, full_shape, jnp.float32), -4.0, 4.0)
    rough = jnp.exp(jax.random.uniform(key_rough, (1, NX, NY, NZ), jnp.float32, 0.0, math.log(10.0)))
    ramp = 1.0 + 2.0 * jnp.arange(NX, dtype=jnp.float32)[None, :, None, None] / max(NX - 1, 1)
    return base * rough * ramp


def block_scale(key, extent, cuts, low, largest):
    loudness, own = 1.0, jax.random.fold_in(key, 6)
    for dim, shards_of in cuts:
        draws = jnp.exp(jax.random.uniform(jax.random.fold_in(own, dim), (shards_of,), jnp.float32, low / len(cuts), largest / len(cuts)))
        loudness = loudness * jnp.repeat(draws, extent[dim] // shards_of).reshape([-1 if axis == dim else 1 for axis in range(len(extent))])
    return loudness


def setup_inputs(seed: int = 0) -> dict:
    seeds = jax.random.split(jax.random.key(seed), 4)
    charges = draw_charges(jax.random.fold_in(seeds[3], 71), 0)
    permittivity = jnp.clip(jnp.exp(math.log(8.0) - 2.0794415 * jax.random.uniform(seeds[1], (NX, NY, NZ), jnp.float32) ** block_scale(seeds[1], (NX, NY, NZ), ((0, 8), (1, 8), (2, 8)), -0.2, 0.2)), 1.0, 8.0)
    screening = jnp.clip(jnp.exp(math.log(2.0) - 3.6888794 * jax.random.uniform(seeds[2], (NX, NY, NZ), jnp.float32) ** block_scale(seeds[2], (NX, NY, NZ), ((0, 8), (1, 8), (2, 8)), -0.2, 0.2)), 0.05, 2.0)
    return {"charges": charges, "permittivity": permittivity, "screening": screening}


shift_value = 20.0
spread_value = 50.0

def apply_operator(padded, eps_pad, screen):
    centre = padded[:, 1:-1, 1:-1, 1:-1]
    eps_mid = eps_pad[1:-1, 1:-1, 1:-1]
    result_sum = screen * centre
    for dimension in range(3):
        length = eps_pad.shape[dimension] - 2
        for offset in (0, 2):
            index_list = [slice(1, -1), slice(1, -1), slice(1, -1)]
            index_list[dimension] = slice(offset, offset + length)
            neighbour = tuple(index_list)
            weight = 0.5 * (eps_mid + eps_pad[neighbour])
            result_sum = result_sum + weight * (centre - padded[(slice(None),) + neighbour])
    return (result_sum - shift_value * centre) / spread_value

def reference(charges, permittivity, screening):
    eps_pad = jnp.pad(permittivity, 1)
    current_block = charges
    blocks = [charges.reshape(NRHS, -1)]
    for power in range(BASIS):
        padded = jnp.pad(current_block, ((0, 0), (1, 1), (1, 1), (1, 1)))
        current_block = apply_operator(padded, eps_pad, screening)
        blocks.append(current_block.reshape(NRHS, -1))
    cell_count = NX * NY * NZ
    rows_list = []
    for first in range(BASIS + 1):
        row_parts = []
        for second in range(BASIS + 1):
            row_parts.append(jnp.dot(blocks[first].astype(jnp.float32), blocks[second].T.astype(jnp.float32), precision=lax.Precision.HIGHEST, preferred_element_type=jnp.float32))
        rows_list.append(jnp.concatenate(row_parts, 1))
    gram = jnp.concatenate(rows_list, 0) / cell_count
    r_factor = jnp.linalg.cholesky(gram).T
    return (current_block, r_factor)
```

```python
import functools

import jax
import jax.numpy as jnp
from jax import lax
from jax.experimental import pallas as pl
from jax.experimental.pallas import tpu as pltpu
from jax.sharding import PartitionSpec as P

MESH = pl.DeviceIdType.MESH
BASIS = 4
NRHS = 8
LANES = 128
MOMENTS = 2 * BASIS + 1
F32 = jnp.float32


def iota(dim):
    return lax.broadcasted_iota(jnp.int32, (8, LANES), dim)


def kernel(dims, ch, eps, scr, top, gram, p, ex, ey, eys, ezs, ezr, wgt, zs, zr, acc,
           sbuf, r1, r2, r3, ssem, rsem, esem, fsem, as1, ar1, as2, ar2, as3, ar3):
    bx, by, nx, ny, nz = dims
    per = LANES // by
    ix, iy, iz = (lax.axis_index(a) for a in ("gx", "gy", "gz"))
    zh = lax.rem(iz, 2)
    zx = lax.div(iz, 2)
    lane, row = iota(1), iota(0)

    faces = (
        (ix < nx - 1, (ix + 1, iy, iz), ix > 0),
        (ix > 0, (ix - 1, iy, iz), ix < nx - 1),
        (iy < ny - 1, (ix, iy + 1, iz), iy > 0),
        (iy > 0, (ix, iy - 1, iz), iy < ny - 1),
        (iz < nz - 1, (ix, iy, iz + 1), iz > 0),
        (iz > 0, (ix, iy, iz - 1), iz < nz - 1),
    )
    n3 = 2 * ny
    me3 = zh * ny + iy

    def peer1(d):
        j = lax.rem(ix + d, nx)
        return j, (j, iy, iz)

    def peer2(d):
        j = lax.rem(zx + d, nz // 2)
        return j, (ix, iy, 2 * j + zh)

    def peer3(d):
        j = lax.rem(me3 + d, n3)
        h = lax.div(j, ny)
        return j, (ix, j - h * ny, 2 * zx + h)

    barrier = pltpu.get_barrier_semaphore()
    count = jnp.int32(0)
    for out, peer, _ in faces:
        @pl.when(out)
        def _():
            pl.semaphore_signal(barrier, inc=1, device_id=peer, device_id_type=MESH)
        count = count + jnp.where(out, 1, 0)
    for n, peer in ((nx, peer1), (nz // 2, peer2), (n3, peer3)):
        @pl.loop(1, n)
        def _(d):
            pl.semaphore_signal(barrier, inc=1, device_id=peer(d)[1], device_id_type=MESH)
        count = count + (n - 1)

    zero = jnp.zeros((8, LANES), F32)

    @pl.loop(0, bx)
    def _(x):
        for y in range(by):
            p[0, x + 1, y + 1] = ch[pl.ds(x * by + y, 8, stride=bx * by), :]
        ex[x + 1] = eps[x]
        ey[x, pl.ds(8, by), :] = eps[x]
        eys[0, pl.ds(x, 1), :] = eps[x, pl.ds(0, 1), :]
        eys[1, pl.ds(x, 1), :] = eps[x, pl.ds(by - 1, 1), :]

    edge = jnp.zeros((by, LANES), F32)

    @pl.when(ix == 0)
    def _():
        ex[0] = edge

        @pl.loop(0, BASIS)
        def _(k):
            for y in range(by):
                p[k, 0, y + 1] = zero

    @pl.when(ix == nx - 1)
    def _():
        ex[bx + 1] = edge

        @pl.loop(0, BASIS)
        def _(k):
            for y in range(by):
                p[k, bx + 1, y + 1] = zero

    @pl.when(iy == 0)
    def _():
        ey[pl.ds(bx, 1)] = jnp.zeros((1, by + 16, LANES), F32)

        @pl.loop(0, BASIS)
        def _(k):
            for x in range(bx):
                p[k, x + 1, 0] = zero

    @pl.when(iy == ny - 1)
    def _():
        ey[pl.ds(bx + 1, 1)] = jnp.zeros((1, by + 16, LANES), F32)

        @pl.loop(0, BASIS)
        def _(k):
            for x in range(bx):
                p[k, x + 1, by + 1] = zero

    @pl.when(iz == 0)
    def _():
        ezr[0] = edge
        zr[:, 0] = jnp.zeros_like(zr[:, 0])

    @pl.when(iz == nz - 1)
    def _():
        ezr[1] = edge
        zr[:, 1] = jnp.zeros_like(zr[:, 1])

    lane_e = lax.broadcasted_iota(jnp.int32, (by, LANES), 1)
    ezs[...] = jnp.zeros_like(ezs)

    @pl.loop(0, bx)
    def _(x):
        e = eps[x]
        ezs[0] = jnp.where(lane_e == x, pltpu.roll(e, x, 1), ezs[0])
        ezs[1] = jnp.where(lane_e == x, pltpu.roll(e, x + 1, 1), ezs[1])

    def pack(k):
        @pl.loop(0, bx)
        def _(x):
            half = lax.div(x, per)
            shift = lax.rem(x, per) * by
            lo = hi = zero
            for y in range(by):
                v = p[k, x + 1, y + 1]
                lo = jnp.where(lane == y, pltpu.roll(v, y, 1), lo)
                hi = jnp.where(lane == y, pltpu.roll(v, y + 1, 1), hi)
            here = (lane >= shift) & (lane < shift + by)
            zs[k, 0, half] = jnp.where(here, pltpu.roll(lo, shift, 1), zs[k, 0, half])
            zs[k, 1, half] = jnp.where(here, pltpu.roll(hi, shift, 1), zs[k, 1, half])

    zs[...] = jnp.zeros_like(zs)
    pack(0)

    pl.semaphore_wait(barrier, count)

    def field(k, i):
        src, dst = (
            (p.at[k, bx, pl.ds(1, by)], p.at[k, 0, pl.ds(1, by)]),
            (p.at[k, 1, pl.ds(1, by)], p.at[k, bx + 1, pl.ds(1, by)]),
            (p.at[k, pl.ds(1, bx), by], p.at[k, pl.ds(1, bx), 0]),
            (p.at[k, pl.ds(1, bx), 1], p.at[k, pl.ds(1, bx), by + 1]),
            (zs.at[k, 1], zr.at[k, 0]),
            (zs.at[k, 0], zr.at[k, 1]),
        )[i]
        return pltpu.make_async_remote_copy(
            src_ref=src, dst_ref=dst, send_sem=ssem.at[k, i], recv_sem=rsem.at[k, i],
            device_id=faces[i][1], device_id_type=MESH)

    def coefficient(i):
        src, dst = (
            (ex.at[bx], ex.at[0]),
            (ex.at[1], ex.at[bx + 1]),
            (eys.at[1], ey.at[bx, pl.ds(8, bx)]),
            (eys.at[0], ey.at[bx + 1, pl.ds(8, bx)]),
            (ezs.at[1], ezr.at[0]),
            (ezs.at[0], ezr.at[1]),
        )[i]
        return pltpu.make_async_remote_copy(
            src_ref=src, dst_ref=dst, send_sem=esem.at[i], recv_sem=fsem.at[i],
            device_id=faces[i][1], device_id_type=MESH)

    def start(copies):
        for i in (4, 5, 0, 1, 2, 3):
            @pl.when(faces[i][0])
            def _():
                copies(i).start()

    def arrive(copies):
        for i in range(6):
            @pl.when(faces[i][2])
            def _():
                copies(i).wait_recv()

    def sent(copies):
        for i in range(6):
            @pl.when(faces[i][0])
            def _():
                copies(i).wait_send()

    start(functools.partial(field, 0))
    start(coefficient)

    def moments(k, first):
        def body(x, sums):
            sums = list(sums)
            for y in range(by):
                b = p[k, x + 1, y + 1]
                a = None if first else p[k - 1, x + 1, y + 1]
                for s in range(5):
                    t = b if s == 0 else pltpu.roll(b, s, 0)
                    sums[s] = sums[s] + b * t
                    if not first:
                        sums[5 + s] = sums[5 + s] + a * t
            return tuple(sums)
        sums = lax.fori_loop(0, bx, body, (zero,) * (5 if first else 10))
        for s in range(5):
            acc[2 * k, s] = sums[s]
            if not first:
                acc[2 * k - 1, s] = sums[5 + s]

    moments(0, True)
    arrive(coefficient)

    @pl.loop(0, bx)
    def _(x):
        e = eps[x]
        ey[x, pl.ds(0, 8), :] = jnp.broadcast_to(ey[bx, pl.ds(8 + x, 1), :], (8, LANES))
        ey[x, pl.ds(8 + by, 8), :] = jnp.broadcast_to(ey[bx + 1, pl.ds(8 + x, 1), :], (8, LANES))
        zm = jnp.where(lane_e == 0, pltpu.roll(ezr[0], lax.rem(LANES - x, LANES), 1), pltpu.roll(e, 1, 1))
        zp = jnp.where(lane_e == LANES - 1, pltpu.roll(ezr[1], LANES - 1 - x, 1), pltpu.roll(e, LANES - 1, 1))
        total = scr[x] * 0.02 - 0.4
        near = (ex[x], ex[x + 2], ey[x, pl.ds(7, by), :], ey[x, pl.ds(9, by), :], zm, zp)
        for i, n in enumerate(near):
            w = (e + n) * 0.01
            wgt[i, x] = w
            total = total + w
        wgt[6, x] = total

    @pl.loop(0, BASIS)
    def _(k):
        arrive(functools.partial(field, k))

        @pl.loop(0, bx)
        def _(x):
            shift = lax.rem(x, per) * by
            half = lax.div(x, per)
            lo = pltpu.roll(zr[k, 0, half], lax.rem(LANES - shift, LANES), 1)
            hi = pltpu.roll(zr[k, 1, half], LANES - 1 - shift, 1)
            for y in range(by):
                v = p[k, x + 1, y + 1]
                zm = jnp.where(lane == 0, pltpu.roll(lo, (LANES - y) % LANES, 1), pltpu.roll(v, 1, 1))
                zp = jnp.where(lane == LANES - 1, pltpu.roll(hi, (LANES - y) % LANES, 1), pltpu.roll(v, LANES - 1, 1))
                near = (p[k, x, y + 1], p[k, x + 2, y + 1], p[k, x + 1, y], p[k, x + 1, y + 2], zm, zp)
                w = [jnp.broadcast_to(wgt[i, x, pl.ds(y, 1), :], (8, LANES)) for i in range(7)]
                terms = [w[i] * near[i] for i in range(6)]
                p[k + 1, x + 1, y + 1] = w[6] * v - (((terms[0] + terms[1]) + (terms[2] + terms[3])) + (terms[4] + terms[5]))

        @pl.when(k < BASIS - 1)
        def _():
            pack(k + 1)
            start(functools.partial(field, k + 1))

        moments(k + 1, False)
        sent(functools.partial(field, k))

    sent(coefficient)

    def body(m, s_all):
        for s in range(8):
            part = acc[m, s] if s <= 4 else pltpu.roll(acc[m, 8 - s], s, 0)
            col = jnp.sum(part, axis=1, keepdims=True)
            s_all = jnp.where(lane == 8 * m + ((row - s) & 7), col, s_all)
        return s_all

    total = lax.fori_loop(0, MOMENTS, body, zero)

    for stage, (n, peer, me, slots, send, recv) in enumerate((
        (nx, peer1, ix, r1, as1, ar1), (nz // 2, peer2, zx, r2, as2, ar2), (n3, peer3, me3, r3, as3, ar3))):
        sbuf[stage] = total
        slots[me] = total

        def copy(d, mine):
            j, device = peer(d)
            return pltpu.make_async_remote_copy(
                src_ref=sbuf.at[stage], dst_ref=slots.at[me if mine else j], send_sem=send.at[d],
                recv_sem=recv.at[me if mine else j], device_id=device, device_id_type=MESH)

        @pl.loop(1, n)
        def _(d):
            copy(d, True).start()

        if stage == 0:
            @pl.loop(0, bx)
            def _(x):
                for y in range(by):
                    top[pl.ds(x * by + y, 8, stride=bx * by), :] = p[BASIS, x + 1, y + 1]

        @pl.loop(1, n)
        def _(d):
            copy(d, False).wait_recv()
        parts = [slots[j] for j in range(n)]
        while len(parts) > 1:
            parts = [parts[i] + parts[i + 1] for i in range(0, len(parts) - 1, 2)] + ([parts[-1]] if len(parts) % 2 else [])
        total = parts[0]

        @pl.loop(1, n)
        def _(d):
            copy(d, True).wait_send()

    cells = bx * by * LANES * nx * ny * nz
    total = total * (1.0 / cells)
    for i in range(BASIS + 1):
        gram[pl.ds(8 * i, 8), :] = total if i == 0 else pltpu.roll(total, LANES - 8 * i, 1)


def per_device(sizes, charges, permittivity, screening):
    _, bx, by, bz = charges.shape
    nx, ny, nz = sizes
    dims = (bx, by, nx, ny, nz)
    halves = max(1, bx * by // LANES)
    vmem = pl.BlockSpec(memory_space=pltpu.VMEM)
    dma = pltpu.SemaphoreType.DMA
    top, gram = pl.pallas_call(
        functools.partial(kernel, dims),
        out_shape=(
            jax.ShapeDtypeStruct((NRHS * bx * by, bz), F32),
            jax.ShapeDtypeStruct((8 * (BASIS + 1), LANES), F32),
        ),
        in_specs=[vmem] * 3,
        out_specs=(vmem, vmem),
        scratch_shapes=[
            pltpu.VMEM((BASIS + 1, bx + 2, by + 2, 8, LANES), F32),
            pltpu.VMEM((bx + 2, by, LANES), F32),
            pltpu.VMEM((bx + 2, by + 16, LANES), F32),
            pltpu.VMEM((2, bx, LANES), F32),
            pltpu.VMEM((2, by, LANES), F32),
            pltpu.VMEM((2, by, LANES), F32),
            pltpu.VMEM((7, bx, by, LANES), F32),
            pltpu.VMEM((BASIS, 2, halves, 8, LANES), F32),
            pltpu.VMEM((BASIS, 2, halves, 8, LANES), F32),
            pltpu.VMEM((MOMENTS, 5, 8, LANES), F32),
            pltpu.VMEM((3, 8, LANES), F32),
            pltpu.VMEM((nx, 8, LANES), F32),
            pltpu.VMEM((nz // 2, 8, LANES), F32),
            pltpu.VMEM((2 * ny, 8, LANES), F32),
            dma((BASIS, 6)), dma((BASIS, 6)), dma((6,)), dma((6,)),
            dma((nx,)), dma((nx,)), dma((nz // 2,)), dma((nz // 2,)), dma((2 * ny,)), dma((2 * ny,)),
        ],
        compiler_params=pltpu.CompilerParams(collective_id=0, has_side_effects=True),
    )(charges.reshape(NRHS * bx * by, bz), permittivity, screening)
    columns = NRHS * (BASIS + 1)
    r_factor = jnp.linalg.cholesky(gram[:, :columns]).T
    return top.reshape(NRHS, bx, by, bz), r_factor


def solution(mesh):
    sizes = tuple(mesh.shape[a] for a in ("gx", "gy", "gz"))
    placed = (P(None, "gx", "gy", "gz"), P("gx", "gy", "gz"), P("gx", "gy", "gz"))
    return jax.shard_map(
        functools.partial(per_device, sizes),
        mesh=mesh,
        in_specs=placed,
        out_specs=(P(None, "gx", "gy", "gz"), P()),
        check_vma=False,
    )
```

```python
import functools

import jax
import jax.numpy as jnp
from jax import lax
from jax.experimental import pallas as pl
from jax.experimental.pallas import tpu as pltpu
from jax.sharding import PartitionSpec as P

MESH = pl.DeviceIdType.MESH
BASIS = 4
NRHS = 8
LANES = 128
MOMENTS = 2 * BASIS + 1
F32 = jnp.float32


def iota(dim):
    return lax.broadcasted_iota(jnp.int32, (8, LANES), dim)


def kernel(dims, ch, eps, scr, top, gram, p, ex, ey, eys, wgt, e, inj, yes, yer, sup, rup,
           ce, ie, csend, crecv, ees, eer, wge, acc, sbuf, r1, r2, r3,
           ssem, rsem, xsem, ysem, zsem, tsem, usem, vsem, esem, fsem, gsem, hsem,
           as1, ar1, as2, ar2, as3, ar3):
    bx, by, nx, ny, nz = dims
    ix, iy, iz = (lax.axis_index(a) for a in ("gx", "gy", "gz"))
    zh = lax.rem(iz, 2)
    zx = lax.div(iz, 2)
    lane, row = iota(1), iota(0)
    place = lane & 7
    zero = jnp.zeros((8, LANES), F32)

    faces = (
        (ix < nx - 1, (ix + 1, iy, iz), ix > 0),
        (ix > 0, (ix - 1, iy, iz), ix < nx - 1),
        (iy < ny - 1, (ix, iy + 1, iz), iy > 0),
        (iy > 0, (ix, iy - 1, iz), iy < ny - 1),
        (iz < nz - 1, (ix, iy, iz + 1), iz > 0),
        (iz > 0, (ix, iy, iz - 1), iz < nz - 1),
    )
    n3 = 2 * ny
    me3 = zh * ny + iy

    def peer1(d):
        j = lax.rem(ix + d, nx)
        return j, (j, iy, iz)

    def peer2(d):
        j = lax.rem(zx + d, nz // 2)
        return j, (ix, iy, 2 * j + zh)

    def peer3(d):
        j = lax.rem(me3 + d, n3)
        h = lax.div(j, ny)
        return j, (ix, j - h * ny, 2 * zx + h)

    barrier = pltpu.get_barrier_semaphore()
    count = jnp.int32(0)
    for out, peer, _ in faces:
        @pl.when(out)
        def _():
            pl.semaphore_signal(barrier, inc=1, device_id=peer, device_id_type=MESH)
        count = count + jnp.where(out, 1, 0)
    for n, peer in ((nx, peer1), (nz // 2, peer2), (n3, peer3)):
        @pl.loop(1, n)
        def _(d):
            pl.semaphore_signal(barrier, inc=1, device_id=peer(d)[1], device_id_type=MESH)
        count = count + (n - 1)

    def inject(y):
        return (lane == (8 * y + 8) % LANES) | (lane == (8 * y - 1) % LANES)

    @pl.loop(0, bx)
    def _(x):
        border, beyond = zero, zero
        for y in range(by):
            v = ch[pl.ds(x * by + y, 8, stride=bx * by), :]
            p[0, x + 1, y + 1] = v
            v = pltpu.roll(v, (8 * y + 4) % LANES, 1)
            border = jnp.where((lane >> 3) == y, v, border)
            beyond = jnp.where(inject(y), v, beyond)
        e[0, x + 1, 0] = border
        e[0, x + 1, 1] = border
        inj[0, x] = beyond
        ex[x + 1] = eps[pl.ds(x * by, by), :]
        ey[x, pl.ds(8, by), :] = eps[pl.ds(x * by, by), :]
        eys[0, pl.ds(x, 1), :] = eps[pl.ds(x * by, 1), :]
        eys[1, pl.ds(x, 1), :] = eps[pl.ds(x * by + by - 1, 1), :]

    @pl.loop(0, bx // 2)
    def _(j):
        even, odd = e[0, 2 * j + 1, 0], e[0, 2 * j + 2, 0]
        sup[0, j] = jnp.where(place < 4, even, pltpu.roll(odd, 4, 1))
        sup[1, j] = jnp.where(place < 4, pltpu.roll(even, LANES - 4, 1), odd)

    lane_e = lax.broadcasted_iota(jnp.int32, (bx, LANES), 1)
    row_e = lax.broadcasted_iota(jnp.int32, (bx, LANES), 0)
    place_e = lane_e & 7
    blank = jnp.zeros((bx, LANES), F32)
    c_e, c_s, i_e = blank, blank, blank
    for y in range(by):
        v = pltpu.roll(eps[pl.ds(y, bx, stride=by), :], (8 * y + 4) % LANES, 1)
        u = pltpu.roll(scr[pl.ds(y, bx, stride=by), :], (8 * y + 4) % LANES, 1)
        c_e = jnp.where((lane_e >> 3) == y, v, c_e)
        c_s = jnp.where((lane_e >> 3) == y, u, c_s)
        i_e = jnp.where((lane_e == (8 * y + 8) % LANES) | (lane_e == (8 * y - 1) % LANES), v, i_e)
    ce[0] = c_e
    ce[1] = c_s
    ie[...] = i_e
    csend[0] = jnp.where(place_e < 4, c_e, pltpu.roll(c_s, 4, 1))
    csend[1] = jnp.where(place_e < 4, pltpu.roll(c_s, LANES - 4, 1), c_e)

    edge = jnp.zeros((by, LANES), F32)
    for there, at, ghost in ((ix == 0, 0, 0), (ix == nx - 1, bx + 1, 1)):
        @pl.when(there)
        def _():
            ex[at] = edge
            for side in range(2):
                eer[ghost, side] = blank

            @pl.loop(0, BASIS)
            def _(k):
                for y in range(by):
                    p[k, at, y + 1] = zero
                e[k, at, 0] = zero
                e[k, at, 1] = zero

    for there, at, ghost in ((iy == 0, 0, 0), (iy == ny - 1, by + 1, 1)):
        @pl.when(there)
        def _():
            ey[pl.ds(bx + ghost, 1)] = jnp.zeros((1, by + 16, LANES), F32)
            for side in range(2):
                eer[2 + ghost, side] = blank

            @pl.loop(0, BASIS)
            def _(k):
                for x in range(bx):
                    p[k, x + 1, at] = zero
                yer[k, ghost, 0] = zero
                yer[k, ghost, 1] = zero

    for there, ghost in ((iz == 0, 0), (iz == nz - 1, 1)):
        @pl.when(there)
        def _():
            crecv[ghost] = blank
            for j in range(bx // 2):
                rup[ghost, j] = zero

    pl.semaphore_wait(barrier, count)

    def remote(src, dst, send, recv, i):
        return pltpu.make_async_remote_copy(
            src_ref=src, dst_ref=dst, send_sem=send, recv_sem=recv, device_id=faces[i][1], device_id_type=MESH)

    def field(k):
        pairs = (
            (p.at[k, bx, pl.ds(1, by)], p.at[k, 0, pl.ds(1, by)]),
            (p.at[k, 1, pl.ds(1, by)], p.at[k, bx + 1, pl.ds(1, by)]),
            (p.at[k, pl.ds(1, bx), by], p.at[k, pl.ds(1, bx), 0]),
            (p.at[k, pl.ds(1, bx), 1], p.at[k, pl.ds(1, bx), by + 1]),
        )
        return [(i, remote(*pairs[i], ssem.at[k, i], rsem.at[k, i], i)) for i in range(4)]

    def rim(k):
        pairs = (
            (e.at[k, bx], e.at[k, 0]),
            (e.at[k, 1], e.at[k, bx + 1]),
            (yes.at[k, 1], yer.at[k, 0]),
            (yes.at[k, 0], yer.at[k, 1]),
        )
        return [(i, remote(*pairs[i], xsem.at[k, i], ysem.at[k, i], i)) for i in range(4)]

    def far():
        return [(4 + i, remote(sup.at[i], rup.at[i], zsem.at[i], tsem.at[i], 4 + i)) for i in range(2)]

    def far_coefficient():
        return [(4 + i, remote(csend.at[i], crecv.at[i], usem.at[i], vsem.at[i], 4 + i)) for i in range(2)]

    def coefficient():
        pairs = (
            (ex.at[bx], ex.at[0]),
            (ex.at[1], ex.at[bx + 1]),
            (eys.at[1], ey.at[bx, pl.ds(8, bx)]),
            (eys.at[0], ey.at[bx + 1, pl.ds(8, bx)]),
        )
        return [(i, remote(*pairs[i], esem.at[i], fsem.at[i], i)) for i in range(4)]

    def rim_coefficient():
        return [(i, remote(ees, eer.at[i], gsem.at[i], hsem.at[i], i)) for i in range(4)]

    def start(copies):
        for i, c in copies:
            @pl.when(faces[i][0])
            def _():
                c.start()

    def arrive(copies):
        for i, c in copies:
            @pl.when(faces[i][2])
            def _():
                c.wait_recv()

    def sent(copies):
        for i, c in copies:
            @pl.when(faces[i][0])
            def _():
                c.wait_send()

    def moments(k):
        inner = (lane >= BASIS) & (lane < LANES - BASIS)

        def body(x, sums):
            sums = list(sums)
            for y in range(by):
                b = p[k, x + 1, y + 1]
                b = jnp.where(inner, b, 0.0)
                for s in range(5):
                    t = b if s == 0 else pltpu.roll(b, s, 0)
                    sums[s] = sums[s] + b * t
                    if k > 0:
                        sums[5 + s] = sums[5 + s] + p[k - 1, x + 1, y + 1] * t
            return tuple(sums)

        sums = lax.fori_loop(0, bx, body, (zero,) * (10 if k else 5))
        for s in range(5):
            acc[2 * k, s] = sums[s]
            if k > 0:
                acc[2 * k - 1, s] = sums[5 + s]

    def rim_moments(k):
        sums = [acc[2 * k, s] for s in range(5)] + ([acc[2 * k - 1, s] for s in range(5)] if k else [])
        for x in range(bx):
            b = jnp.where(place < 4, e[k, x + 1, 1], e[k, x + 1, 0])
            a = jnp.where(place < 4, e[k - 1, x + 1, 1], e[k - 1, x + 1, 0]) if k else None
            for s in range(5):
                t = b if s == 0 else pltpu.roll(b, s, 0)
                sums[s] = sums[s] + b * t
                if k > 0:
                    sums[5 + s] = sums[5 + s] + a * t
        for s in range(5):
            acc[2 * k, s] = sums[s]
            if k > 0:
                acc[2 * k - 1, s] = sums[5 + s]

    def reduce(first, last, table):
        for m in range(first, last):
            for s in range(8):
                part = acc[m, s] if s <= 4 else pltpu.roll(acc[m, 8 - s], s, 0)
                col = jnp.sum(part, axis=1, keepdims=True)
                table = jnp.where(lane == 8 * m + ((row - s) & 7), col, table)
        return table

    def spread(ref, *at):
        return jnp.broadcast_to(ref[at], (8, LANES))

    def step(k):
        @pl.loop(0, bx)
        def _(x):
            beyond = zero
            for y in range(by):
                v = p[k, x + 1, y + 1]
                near = (p[k, x, y + 1], p[k, x + 2, y + 1], p[k, x + 1, y], p[k, x + 1, y + 2],
                        pltpu.roll(v, 1, 1), pltpu.roll(v, LANES - 1, 1))
                w = [spread(wgt, i, x, pl.ds(y, 1)) for i in range(7)]
                t = [w[i] * near[i] for i in range(6)]
                v = w[6] * v - (((t[0] + t[1]) + (t[2] + t[3])) + (t[4] + t[5]))
                p[k + 1, x + 1, y + 1] = v
                if k < BASIS - 1:
                    beyond = jnp.where(inject(y), pltpu.roll(v, (8 * y + 4) % LANES, 1), beyond)
            if k < BASIS - 1:
                inj[k + 1, x] = beyond

    def rim_edges(k):
        for side in range(2):
            low, high = zero, zero
            for x in range(bx):
                v = e[k, x + 1, side]
                here = (lane >> 3) == x
                low = jnp.where(here, pltpu.roll(v, 8 * x, 1) if x else v, low)
                high = jnp.where(here, pltpu.roll(v, (8 * x + 8) % LANES, 1), high)
            yes[k, 0, side] = low
            yes[k, 1, side] = high

    def rim_step(k):
        for side in range(2):
            before, after = yer[k, 0, side], yer[k, 1, side]
            low, high = zero, zero
            for x in range(bx):
                v = e[k, x + 1, side]
                beyond = inj[k, x]
                ym = jnp.where(lane < 8, pltpu.roll(before, (LANES - 8 * x) % LANES, 1), pltpu.roll(v, 8, 1))
                yp = jnp.where(lane >= LANES - 8, pltpu.roll(after, LANES - 8 - 8 * x, 1), pltpu.roll(v, LANES - 8, 1))
                zm = pltpu.roll(jnp.where(place == 7, beyond, v) if side else v, 1, 1)
                zp = pltpu.roll(v if side else jnp.where(place == 0, beyond, v), LANES - 1, 1)
                near = (e[k, x, side], e[k, x + 2, side], ym, yp, zm, zp)
                w = [spread(wge, i, side, pl.ds(x, 1)) for i in range(7)]
                t = [w[i] * near[i] for i in range(6)]
                v = w[6] * v - (((t[0] + t[1]) + (t[2] + t[3])) + (t[4] + t[5]))
                e[k + 1, x + 1, side] = v
                if k < BASIS - 1:
                    here = (lane >> 3) == x
                    low = jnp.where(here, pltpu.roll(v, 8 * x, 1) if x else v, low)
                    high = jnp.where(here, pltpu.roll(v, (8 * x + 8) % LANES, 1), high)
            if k < BASIS - 1:
                yes[k + 1, 0, side] = low
                yes[k + 1, 1, side] = high

    start(far())
    start(far_coefficient())
    start(field(0))
    start(coefficient())
    moments(0)

    arrive(coefficient())

    @pl.loop(0, bx)
    def _(x):
        c = eps[pl.ds(x * by, by), :]
        ey[x, pl.ds(0, 8), :] = spread(ey, bx, pl.ds(8 + x, 1))
        ey[x, pl.ds(8 + by, 8), :] = spread(ey, bx + 1, pl.ds(8 + x, 1))
        total = scr[pl.ds(x * by, by), :] * 0.02 - 0.4
        near = (ex[x], ex[x + 2], ey[x, pl.ds(7, by), :], ey[x, pl.ds(9, by), :],
                pltpu.roll(c, 1, 1), pltpu.roll(c, LANES - 1, 1))
        for i, n in enumerate(near):
            w = (c + n) * 0.01
            wgt[i, x] = w
            total = total + w
        wgt[6, x] = total

    arrive(field(0))
    step(0)
    start(field(1))
    moments(1)
    arrive(field(1))
    step(1)
    start(field(2))

    arrive(far())
    arrive(far_coefficient())

    @pl.loop(0, bx // 2)
    def _(j):
        even, odd = e[0, 2 * j + 1, 0], e[0, 2 * j + 2, 0]
        lo, hi = rup[0, j], rup[1, j]
        e[0, 2 * j + 1, 0] = jnp.where(place < 4, lo, even)
        e[0, 2 * j + 2, 0] = jnp.where(place < 4, pltpu.roll(lo, LANES - 4, 1), odd)
        e[0, 2 * j + 1, 1] = jnp.where(place < 4, even, pltpu.roll(hi, 4, 1))
        e[0, 2 * j + 2, 1] = jnp.where(place < 4, odd, hi)

    rim_edges(0)
    c_e, c_s = ce[0], ce[1]
    e_side = (jnp.where(place_e < 4, crecv[0], c_e), jnp.where(place_e < 4, c_e, crecv[1]))
    s_side = (jnp.where(place_e < 4, pltpu.roll(crecv[0], LANES - 4, 1), c_s),
              jnp.where(place_e < 4, c_s, pltpu.roll(crecv[1], 4, 1)))
    ees[0] = e_side[0]
    ees[1] = e_side[1]
    start(rim_coefficient())
    start(rim(0))

    moments(2)
    arrive(field(2))
    step(2)
    start(field(3))

    arrive(rim_coefficient())
    for side in range(2):
        c, beyond = ees[side], ie[...]
        xm = jnp.where(row_e == 0, pltpu.roll(eer[0, side], 1, 0), pltpu.roll(c, 1, 0))
        xp = jnp.where(row_e == bx - 1, pltpu.roll(eer[1, side], bx - 1, 0), pltpu.roll(c, bx - 1, 0))
        ym = jnp.where(lane_e < 8, pltpu.roll(eer[2, side], 8, 1), pltpu.roll(c, 8, 1))
        yp = jnp.where(lane_e >= LANES - 8, pltpu.roll(eer[3, side], LANES - 8, 1), pltpu.roll(c, LANES - 8, 1))
        zm = pltpu.roll(jnp.where(place_e == 7, beyond, c) if side else c, 1, 1)
        zp = pltpu.roll(c if side else jnp.where(place_e == 0, beyond, c), LANES - 1, 1)
        if side:
            inside = (place_e < 4) | (iz < nz - 1)
        else:
            inside = (place_e >= 4) | (iz > 0)
        total = s_side[side] * 0.02 - 0.4
        for i, n in enumerate((xm, xp, ym, yp, zm, zp)):
            w = (c + n) * 0.01
            wge[i, side] = jnp.where(inside, w, 0.0)
            total = total + w
        wge[6, side] = jnp.where(inside, total, 0.0)

    arrive(rim(0))
    rim_step(0)
    start(rim(1))
    arrive(field(3))
    step(3)
    arrive(rim(1))
    rim_step(1)
    start(rim(2))
    moments(3)
    arrive(rim(2))
    rim_step(2)
    start(rim(3))
    moments(4)
    for k in range(BASIS):
        rim_moments(k)
    table = reduce(0, 2 * BASIS - 1, zero)
    arrive(rim(3))
    rim_step(3)
    rim_moments(BASIS)
    total = reduce(2 * BASIS - 1, MOMENTS, table)

    for stage, (n, peer, me, slots, send, recv) in enumerate((
        (nx, peer1, ix, r1, as1, ar1), (nz // 2, peer2, zx, r2, as2, ar2), (n3, peer3, me3, r3, as3, ar3))):
        sbuf[stage] = total
        slots[me] = total

        def copy(d, mine):
            j, device = peer(d)
            return pltpu.make_async_remote_copy(
                src_ref=sbuf.at[stage], dst_ref=slots.at[me if mine else j], send_sem=send.at[d],
                recv_sem=recv.at[me if mine else j], device_id=device, device_id_type=MESH)

        @pl.loop(1, n)
        def _(d):
            copy(d, True).start()

        if stage == 0:
            for k in range(BASIS):
                sent(field(k))
                sent(rim(k))
            for c in (far(), far_coefficient(), coefficient(), rim_coefficient()):
                sent(c)

        if stage == 2:
            @pl.loop(0, bx)
            def _(x):
                border = jnp.where(place < 4, e[BASIS, x + 1, 1], e[BASIS, x + 1, 0])
                inner = (lane >= BASIS) & (lane < LANES - BASIS)
                for y in range(by):
                    v = jnp.where(inner, p[BASIS, x + 1, y + 1], pltpu.roll(border, (LANES - 4 - 8 * y) % LANES, 1))
                    top[pl.ds(x * by + y, 8, stride=bx * by), :] = v

        @pl.loop(1, n)
        def _(d):
            copy(d, False).wait_recv()
        parts = [slots[j] for j in range(n)]
        while len(parts) > 1:
            parts = [parts[i] + parts[i + 1] for i in range(0, len(parts) - 1, 2)] + ([parts[-1]] if len(parts) % 2 else [])
        total = parts[0]

        @pl.loop(1, n)
        def _(d):
            copy(d, True).wait_send()

    cells = bx * by * LANES * nx * ny * nz
    total = total * (1.0 / cells)
    for i in range(BASIS + 1):
        gram[pl.ds(8 * i, 8), :] = total if i == 0 else pltpu.roll(total, LANES - 8 * i, 1)


def per_device(sizes, charges, permittivity, screening):
    _, bx, by, bz = charges.shape
    nx, ny, nz = sizes
    dims = (bx, by, nx, ny, nz)
    vmem = pl.BlockSpec(memory_space=pltpu.VMEM)
    dma = pltpu.SemaphoreType.DMA

    def buf(*shape):
        return pltpu.VMEM(shape, F32)

    tile = (8, LANES)
    top, gram = pl.pallas_call(
        functools.partial(kernel, dims),
        out_shape=(
            jax.ShapeDtypeStruct((NRHS * bx * by, bz), F32),
            jax.ShapeDtypeStruct((8 * (BASIS + 1), LANES), F32),
        ),
        in_specs=[vmem] * 3,
        out_specs=(vmem, vmem),
        scratch_shapes=[
            buf(BASIS + 1, bx + 2, by + 2, *tile),
            buf(bx + 2, by, LANES),
            buf(bx + 2, by + 16, LANES),
            buf(2, bx, LANES),
            buf(7, bx, by, LANES),
            buf(BASIS + 1, bx + 2, 2, *tile),
            buf(BASIS, bx, *tile),
            buf(BASIS, 2, 2, *tile), buf(BASIS, 2, 2, *tile),
            buf(2, bx // 2, *tile), buf(2, bx // 2, *tile),
            buf(2, bx, LANES), buf(bx, LANES),
            buf(2, bx, LANES), buf(2, bx, LANES),
            buf(2, bx, LANES), buf(4, 2, bx, LANES),
            buf(7, 2, bx, LANES),
            buf(MOMENTS, 5, *tile),
            buf(3, *tile), buf(nx, *tile), buf(nz // 2, *tile), buf(2 * ny, *tile),
            dma((BASIS, 4)), dma((BASIS, 4)), dma((BASIS, 4)), dma((BASIS, 4)),
            dma((2,)), dma((2,)), dma((2,)), dma((2,)), dma((4,)), dma((4,)), dma((4,)), dma((4,)),
            dma((nx,)), dma((nx,)), dma((nz // 2,)), dma((nz // 2,)), dma((2 * ny,)), dma((2 * ny,)),
        ],
        compiler_params=pltpu.CompilerParams(collective_id=0, has_side_effects=True),
    )(charges.reshape(NRHS * bx * by, bz), permittivity.reshape(bx * by, bz), screening.reshape(bx * by, bz))
    columns = NRHS * (BASIS + 1)
    r_factor = jnp.linalg.cholesky(gram[:, :columns]).T
    return top.reshape(NRHS, bx, by, bz), r_factor


def solution(mesh):
    sizes = tuple(mesh.shape[a] for a in ("gx", "gy", "gz"))
    placed = (P(None, "gx", "gy", "gz"), P("gx", "gy", "gz"), P("gx", "gy", "gz"))
    return jax.shard_map(
        functools.partial(per_device, sizes),
        mesh=mesh,
        in_specs=placed,
        out_specs=(P(None, "gx", "gy", "gz"), P()),
        check_vma=False,
    )
```

```python
import functools

import jax
import jax.numpy as jnp
from jax import lax
from jax.experimental import pallas as pl
from jax.experimental.pallas import tpu as pltpu
from jax.sharding import PartitionSpec as P

MESH = pl.DeviceIdType.MESH
BASIS = 4
NRHS = 8
LANES = 128
MOMENTS = 2 * BASIS + 1
F32 = jnp.float32


def iota(dim):
    return lax.broadcasted_iota(jnp.int32, (8, LANES), dim)


def kernel(dims, ch_in, eps_in, scr_in, top, gram, ch, eps, scr, insem, p, ex, ey, eys, wgt, e, inj, yes, yer, sup, rup,
           ce, ie, csend, crecv, ees, eer, wge, acc, sbuf, r1, r2, r3,
           ssem, rsem, xsem, ysem, zsem, tsem, usem, vsem, esem, fsem, gsem, hsem,
           as1, ar1, as2, ar2, as3, ar3):
    bx, by, nx, ny, nz = dims
    ix, iy, iz = (lax.axis_index(a) for a in ("gx", "gy", "gz"))
    zh = lax.rem(iz, 2)
    zx = lax.div(iz, 2)
    lane, row = iota(1), iota(0)
    place = lane & 7
    zero = jnp.zeros((8, LANES), F32)

    faces = (
        (ix < nx - 1, (ix + 1, iy, iz), ix > 0),
        (ix > 0, (ix - 1, iy, iz), ix < nx - 1),
        (iy < ny - 1, (ix, iy + 1, iz), iy > 0),
        (iy > 0, (ix, iy - 1, iz), iy < ny - 1),
        (iz < nz - 1, (ix, iy, iz + 1), iz > 0),
        (iz > 0, (ix, iy, iz - 1), iz < nz - 1),
    )
    n3 = 2 * ny
    me3 = zh * ny + iy

    def peer1(d):
        j = lax.rem(ix + d, nx)
        return j, (j, iy, iz)

    def peer2(d):
        j = lax.rem(zx + d, nz // 2)
        return j, (ix, iy, 2 * j + zh)

    def peer3(d):
        j = lax.rem(me3 + d, n3)
        h = lax.div(j, ny)
        return j, (ix, j - h * ny, 2 * zx + h)

    loads = [pltpu.make_async_copy(src, dst, insem.at[i])
             for i, (src, dst) in enumerate(((ch_in, ch), (eps_in, eps), (scr_in, scr)))]
    for c in loads:
        c.start()

    barrier = pltpu.get_barrier_semaphore()
    count = jnp.int32(0)
    for out, peer, _ in faces[4:]:
        @pl.when(out)
        def _():
            pl.semaphore_signal(barrier, inc=1, device_id=peer, device_id_type=MESH)
        count = count + jnp.where(out, 1, 0)
    for n, peer in ((n3, peer3), (nx, peer1), (nz // 2, peer2)):
        @pl.loop(1, n)
        def _(d):
            pl.semaphore_signal(barrier, inc=1, device_id=peer(d)[1], device_id_type=MESH)
        count = count + (n - 1)

    for c in loads:
        c.wait()

    def inject(y):
        return (lane == (8 * y + 8) % LANES) | (lane == (8 * y - 1) % LANES)

    @pl.loop(0, bx)
    def _(x):
        border, beyond = zero, zero
        for y in range(by):
            v = ch[pl.ds(x * by + y, 8, stride=bx * by), :]
            p[0, x + 1, y + 1] = v
            v = pltpu.roll(v, (8 * y + 4) % LANES, 1)
            border = jnp.where((lane >> 3) == y, v, border)
            beyond = jnp.where(inject(y), v, beyond)
        e[0, x + 1, 0] = border
        e[0, x + 1, 1] = border
        inj[0, x] = beyond
        ex[x + 1] = eps[pl.ds(x * by, by), :]
        ey[x, pl.ds(8, by), :] = eps[pl.ds(x * by, by), :]
        eys[0, pl.ds(x, 1), :] = eps[pl.ds(x * by, 1), :]
        eys[1, pl.ds(x, 1), :] = eps[pl.ds(x * by + by - 1, 1), :]

    @pl.loop(0, bx // 2)
    def _(j):
        even, odd = e[0, 2 * j + 1, 0], e[0, 2 * j + 2, 0]
        sup[0, j] = jnp.where(place < 4, even, pltpu.roll(odd, 4, 1))
        sup[1, j] = jnp.where(place < 4, pltpu.roll(even, LANES - 4, 1), odd)

    lane_e = lax.broadcasted_iota(jnp.int32, (bx, LANES), 1)
    row_e = lax.broadcasted_iota(jnp.int32, (bx, LANES), 0)
    place_e = lane_e & 7
    blank = jnp.zeros((bx, LANES), F32)
    c_e, c_s, i_e = blank, blank, blank
    for y in range(by):
        v = pltpu.roll(eps[pl.ds(y, bx, stride=by), :], (8 * y + 4) % LANES, 1)
        u = pltpu.roll(scr[pl.ds(y, bx, stride=by), :], (8 * y + 4) % LANES, 1)
        c_e = jnp.where((lane_e >> 3) == y, v, c_e)
        c_s = jnp.where((lane_e >> 3) == y, u, c_s)
        i_e = jnp.where((lane_e == (8 * y + 8) % LANES) | (lane_e == (8 * y - 1) % LANES), v, i_e)
    ce[0] = c_e
    ce[1] = c_s
    ie[...] = i_e
    csend[0] = jnp.where(place_e < 4, c_e, pltpu.roll(c_s, 4, 1))
    csend[1] = jnp.where(place_e < 4, pltpu.roll(c_s, LANES - 4, 1), c_e)

    edge = jnp.zeros((by, LANES), F32)
    for there, at, ghost in ((ix == 0, 0, 0), (ix == nx - 1, bx + 1, 1)):
        @pl.when(there)
        def _():
            ex[at] = edge
            for side in range(2):
                eer[ghost, side] = blank

            @pl.loop(0, BASIS)
            def _(k):
                for y in range(by):
                    p[k, at, y + 1] = zero
                e[k, at, 0] = zero
                e[k, at, 1] = zero

    for there, at, ghost in ((iy == 0, 0, 0), (iy == ny - 1, by + 1, 1)):
        @pl.when(there)
        def _():
            ey[pl.ds(bx + ghost, 1)] = jnp.zeros((1, by + 16, LANES), F32)
            for side in range(2):
                eer[2 + ghost, side] = blank

            @pl.loop(0, BASIS)
            def _(k):
                for x in range(bx):
                    p[k, x + 1, at] = zero
                yer[k, ghost, 0] = zero
                yer[k, ghost, 1] = zero

    for there, ghost in ((iz == 0, 0), (iz == nz - 1, 1)):
        @pl.when(there)
        def _():
            crecv[ghost] = blank
            for j in range(bx // 2):
                rup[ghost, j] = zero

    pl.semaphore_wait(barrier, count)

    def remote(src, dst, send, recv, i):
        return pltpu.make_async_remote_copy(
            src_ref=src, dst_ref=dst, send_sem=send, recv_sem=recv, device_id=faces[i][1], device_id_type=MESH)

    def field(k):
        pairs = (
            (p.at[k, bx, pl.ds(1, by)], p.at[k, 0, pl.ds(1, by)]),
            (p.at[k, 1, pl.ds(1, by)], p.at[k, bx + 1, pl.ds(1, by)]),
            (p.at[k, pl.ds(1, bx), by], p.at[k, pl.ds(1, bx), 0]),
            (p.at[k, pl.ds(1, bx), 1], p.at[k, pl.ds(1, bx), by + 1]),
        )
        return [(i, remote(*pairs[i], ssem.at[k, i], rsem.at[k, i], i)) for i in range(4)]

    def rim(k):
        pairs = (
            (e.at[k, bx], e.at[k, 0]),
            (e.at[k, 1], e.at[k, bx + 1]),
            (yes.at[k, 1], yer.at[k, 0]),
            (yes.at[k, 0], yer.at[k, 1]),
        )
        return [(i, remote(*pairs[i], xsem.at[k, i], ysem.at[k, i], i)) for i in range(4)]

    def far():
        return [(4 + i, remote(sup.at[i], rup.at[i], zsem.at[i], tsem.at[i], 4 + i)) for i in range(2)]

    def far_coefficient():
        return [(4 + i, remote(csend.at[i], crecv.at[i], usem.at[i], vsem.at[i], 4 + i)) for i in range(2)]

    def coefficient():
        pairs = (
            (ex.at[bx], ex.at[0]),
            (ex.at[1], ex.at[bx + 1]),
            (eys.at[1], ey.at[bx, pl.ds(8, bx)]),
            (eys.at[0], ey.at[bx + 1, pl.ds(8, bx)]),
        )
        return [(i, remote(*pairs[i], esem.at[i], fsem.at[i], i)) for i in range(4)]

    def rim_coefficient():
        return [(i, remote(ees, eer.at[i], gsem.at[i], hsem.at[i], i)) for i in range(4)]

    def start(copies):
        for i, c in copies:
            @pl.when(faces[i][0])
            def _():
                c.start()

    def arrive(copies):
        for i, c in copies:
            @pl.when(faces[i][2])
            def _():
                c.wait_recv()

    def sent(copies):
        for i, c in copies:
            @pl.when(faces[i][0])
            def _():
                c.wait_send()

    def moments(k):
        inner = (lane >= BASIS) & (lane < LANES - BASIS)

        def body(x, sums):
            sums = list(sums)
            for y in range(by):
                b = p[k, x + 1, y + 1]
                b = jnp.where(inner, b, 0.0)
                for s in range(5):
                    t = b if s == 0 else pltpu.roll(b, s, 0)
                    sums[s] = sums[s] + b * t
                    if k > 0:
                        sums[5 + s] = sums[5 + s] + p[k - 1, x + 1, y + 1] * t
            return tuple(sums)

        sums = lax.fori_loop(0, bx, body, (zero,) * (10 if k else 5))
        for s in range(5):
            acc[2 * k, s] = sums[s]
            if k > 0:
                acc[2 * k - 1, s] = sums[5 + s]

    def rim_moments(k):
        sums = [acc[2 * k, s] for s in range(5)] + ([acc[2 * k - 1, s] for s in range(5)] if k else [])
        for x in range(bx):
            b = jnp.where(place < 4, e[k, x + 1, 1], e[k, x + 1, 0])
            a = jnp.where(place < 4, e[k - 1, x + 1, 1], e[k - 1, x + 1, 0]) if k else None
            for s in range(5):
                t = b if s == 0 else pltpu.roll(b, s, 0)
                sums[s] = sums[s] + b * t
                if k > 0:
                    sums[5 + s] = sums[5 + s] + a * t
        for s in range(5):
            acc[2 * k, s] = sums[s]
            if k > 0:
                acc[2 * k - 1, s] = sums[5 + s]

    def reduce(first, last, table):
        for m in range(first, last):
            for s in range(8):
                part = acc[m, s] if s <= 4 else pltpu.roll(acc[m, 8 - s], s, 0)
                col = jnp.sum(part, axis=1, keepdims=True)
                table = jnp.where(lane == 8 * m + ((row - s) & 7), col, table)
        return table

    def spread(ref, *at):
        return jnp.broadcast_to(ref[at], (8, LANES))

    def cells(k, x, ys, beyond):
        for y in ys:
            v = p[k, x + 1, y + 1]
            near = (p[k, x, y + 1], p[k, x + 2, y + 1], p[k, x + 1, y], p[k, x + 1, y + 2],
                    pltpu.roll(v, 1, 1), pltpu.roll(v, LANES - 1, 1))
            w = [spread(wgt, i, x, pl.ds(y, 1)) for i in range(7)]
            t = [w[i] * near[i] for i in range(6)]
            v = w[6] * v - (((t[0] + t[1]) + (t[2] + t[3])) + (t[4] + t[5]))
            p[k + 1, x + 1, y + 1] = v
            if k < BASIS - 1:
                beyond = jnp.where(inject(y), pltpu.roll(v, (8 * y + 4) % LANES, 1), beyond)
        if k < BASIS - 1:
            inj[k + 1, x] = beyond

    def interior(k):
        @pl.loop(1, bx - 1)
        def _(x):
            cells(k, x, range(1, by - 1), zero)

    def border(k):
        @pl.loop(0, 2)
        def _(j):
            cells(k, j * (bx - 1), range(by), zero)

        @pl.loop(0, 2)
        def _(j):
            for i in range(bx // 2 - 1):
                x = 1 + j * (bx // 2 - 1) + i
                cells(k, x, (0, by - 1), inj[k + 1, x] if k < BASIS - 1 else zero)

    def rim_edges(k):
        for side in range(2):
            low, high = zero, zero
            for x in range(bx):
                v = e[k, x + 1, side]
                here = (lane >> 3) == x
                low = jnp.where(here, pltpu.roll(v, 8 * x, 1) if x else v, low)
                high = jnp.where(here, pltpu.roll(v, (8 * x + 8) % LANES, 1), high)
            yes[k, 0, side] = low
            yes[k, 1, side] = high

    def rim_step(k):
        for side in range(2):
            before, after = yer[k, 0, side], yer[k, 1, side]
            low, high = zero, zero
            for x in range(bx):
                v = e[k, x + 1, side]
                beyond = inj[k, x]
                ym = jnp.where(lane < 8, pltpu.roll(before, (LANES - 8 * x) % LANES, 1), pltpu.roll(v, 8, 1))
                yp = jnp.where(lane >= LANES - 8, pltpu.roll(after, LANES - 8 - 8 * x, 1), pltpu.roll(v, LANES - 8, 1))
                zm = pltpu.roll(jnp.where(place == 7, beyond, v) if side else v, 1, 1)
                zp = pltpu.roll(v if side else jnp.where(place == 0, beyond, v), LANES - 1, 1)
                near = (e[k, x, side], e[k, x + 2, side], ym, yp, zm, zp)
                w = [spread(wge, i, side, pl.ds(x, 1)) for i in range(7)]
                t = [w[i] * near[i] for i in range(6)]
                v = w[6] * v - (((t[0] + t[1]) + (t[2] + t[3])) + (t[4] + t[5]))
                e[k + 1, x + 1, side] = v
                if k < BASIS - 1:
                    here = (lane >> 3) == x
                    low = jnp.where(here, pltpu.roll(v, 8 * x, 1) if x else v, low)
                    high = jnp.where(here, pltpu.roll(v, (8 * x + 8) % LANES, 1), high)
            if k < BASIS - 1:
                yes[k + 1, 0, side] = low
                yes[k + 1, 1, side] = high

    start(coefficient())
    start(far())
    start(far_coefficient())
    start(field(0))
    moments(0)

    arrive(coefficient())

    @pl.loop(0, bx)
    def _(x):
        c = eps[pl.ds(x * by, by), :]
        ey[x, pl.ds(0, 8), :] = spread(ey, bx, pl.ds(8 + x, 1))
        ey[x, pl.ds(8 + by, 8), :] = spread(ey, bx + 1, pl.ds(8 + x, 1))
        total = scr[pl.ds(x * by, by), :] * 0.02 - 0.4
        near = (ex[x], ex[x + 2], ey[x, pl.ds(7, by), :], ey[x, pl.ds(9, by), :],
                pltpu.roll(c, 1, 1), pltpu.roll(c, LANES - 1, 1))
        for i, n in enumerate(near):
            w = (c + n) * 0.01
            wgt[i, x] = w
            total = total + w
        wgt[6, x] = total

    interior(0)
    arrive(field(0))
    border(0)
    start(field(1))
    interior(1)
    moments(1)
    arrive(field(1))
    border(1)
    start(field(2))
    interior(2)

    arrive(far())
    arrive(far_coefficient())

    @pl.loop(0, bx // 2)
    def _(j):
        even, odd = e[0, 2 * j + 1, 0], e[0, 2 * j + 2, 0]
        lo, hi = rup[0, j], rup[1, j]
        e[0, 2 * j + 1, 0] = jnp.where(place < 4, lo, even)
        e[0, 2 * j + 2, 0] = jnp.where(place < 4, pltpu.roll(lo, LANES - 4, 1), odd)
        e[0, 2 * j + 1, 1] = jnp.where(place < 4, even, pltpu.roll(hi, 4, 1))
        e[0, 2 * j + 2, 1] = jnp.where(place < 4, odd, hi)

    rim_edges(0)
    c_e, c_s = ce[0], ce[1]
    e_side = (jnp.where(place_e < 4, crecv[0], c_e), jnp.where(place_e < 4, c_e, crecv[1]))
    s_side = (jnp.where(place_e < 4, pltpu.roll(crecv[0], LANES - 4, 1), c_s),
              jnp.where(place_e < 4, c_s, pltpu.roll(crecv[1], 4, 1)))
    ees[0] = e_side[0]
    ees[1] = e_side[1]
    start(rim_coefficient())
    start(rim(0))
    moments(2)

    arrive(rim_coefficient())
    for side in range(2):
        c, beyond = ees[side], ie[...]
        xm = jnp.where(row_e == 0, pltpu.roll(eer[0, side], 1, 0), pltpu.roll(c, 1, 0))
        xp = jnp.where(row_e == bx - 1, pltpu.roll(eer[1, side], bx - 1, 0), pltpu.roll(c, bx - 1, 0))
        ym = jnp.where(lane_e < 8, pltpu.roll(eer[2, side], 8, 1), pltpu.roll(c, 8, 1))
        yp = jnp.where(lane_e >= LANES - 8, pltpu.roll(eer[3, side], LANES - 8, 1), pltpu.roll(c, LANES - 8, 1))
        zm = pltpu.roll(jnp.where(place_e == 7, beyond, c) if side else c, 1, 1)
        zp = pltpu.roll(c if side else jnp.where(place_e == 0, beyond, c), LANES - 1, 1)
        if side:
            inside = (place_e < 4) | (iz < nz - 1)
        else:
            inside = (place_e >= 4) | (iz > 0)
        total = s_side[side] * 0.02 - 0.4
        for i, n in enumerate((xm, xp, ym, yp, zm, zp)):
            w = (c + n) * 0.01
            wge[i, side] = jnp.where(inside, w, 0.0)
            total = total + w
        wge[6, side] = jnp.where(inside, total, 0.0)

    arrive(rim(0))
    rim_step(0)
    start(rim(1))
    arrive(field(2))
    border(2)
    start(field(3))
    arrive(rim(1))
    rim_step(1)
    start(rim(2))
    interior(3)
    moments(3)
    arrive(rim(2))
    rim_step(2)
    start(rim(3))
    arrive(field(3))
    border(3)
    moments(4)
    for k in range(BASIS):
        rim_moments(k)
    table = reduce(0, 2 * BASIS - 1, zero)
    arrive(rim(3))
    rim_step(3)
    rim_moments(BASIS)
    total = reduce(2 * BASIS - 1, MOMENTS, table)

    for stage, (n, peer, me, slots, send, recv) in enumerate((
        (nx, peer1, ix, r1, as1, ar1), (nz // 2, peer2, zx, r2, as2, ar2), (n3, peer3, me3, r3, as3, ar3))):
        sbuf[stage] = total
        slots[me] = total

        def copy(d, mine):
            j, device = peer(d)
            return pltpu.make_async_remote_copy(
                src_ref=sbuf.at[stage], dst_ref=slots.at[me if mine else j], send_sem=send.at[d],
                recv_sem=recv.at[me if mine else j], device_id=device, device_id_type=MESH)

        @pl.loop(1, n)
        def _(d):
            copy(d, True).start()

        if stage == 0:
            for k in range(BASIS):
                sent(field(k))
                sent(rim(k))
            for c in (far(), far_coefficient(), coefficient(), rim_coefficient()):
                sent(c)

        if stage == 2:
            @pl.loop(0, bx)
            def _(x):
                border = jnp.where(place < 4, e[BASIS, x + 1, 1], e[BASIS, x + 1, 0])
                inner = (lane >= BASIS) & (lane < LANES - BASIS)
                for y in range(by):
                    v = jnp.where(inner, p[BASIS, x + 1, y + 1], pltpu.roll(border, (LANES - 4 - 8 * y) % LANES, 1))
                    top[pl.ds(x * by + y, 8, stride=bx * by), :] = v

        @pl.loop(1, n)
        def _(d):
            copy(d, False).wait_recv()
        parts = [slots[j] for j in range(n)]
        while len(parts) > 1:
            parts = [parts[i] + parts[i + 1] for i in range(0, len(parts) - 1, 2)] + ([parts[-1]] if len(parts) % 2 else [])
        total = parts[0]

        @pl.loop(1, n)
        def _(d):
            copy(d, True).wait_send()

    cells = bx * by * LANES * nx * ny * nz
    total = total * (1.0 / cells)
    for i in range(BASIS + 1):
        gram[pl.ds(8 * i, 8), :] = total if i == 0 else pltpu.roll(total, LANES - 8 * i, 1)


def per_device(sizes, charges, permittivity, screening):
    _, bx, by, bz = charges.shape
    nx, ny, nz = sizes
    dims = (bx, by, nx, ny, nz)
    vmem = pl.BlockSpec(memory_space=pltpu.VMEM)
    dma = pltpu.SemaphoreType.DMA

    def buf(*shape):
        return pltpu.VMEM(shape, F32)

    tile = (8, LANES)
    top, gram = pl.pallas_call(
        functools.partial(kernel, dims),
        out_shape=(
            jax.ShapeDtypeStruct((NRHS * bx * by, bz), F32),
            jax.ShapeDtypeStruct((8 * (BASIS + 1), LANES), F32),
        ),
        in_specs=[pl.BlockSpec(memory_space=pltpu.HBM)] * 3,
        out_specs=(vmem, vmem),
        scratch_shapes=[
            buf(NRHS * bx * by, LANES), buf(bx * by, LANES), buf(bx * by, LANES),
            dma((3,)),
            buf(BASIS + 1, bx + 2, by + 2, *tile),
            buf(bx + 2, by, LANES),
            buf(bx + 2, by + 16, LANES),
            buf(2, bx, LANES),
            buf(7, bx, by, LANES),
            buf(BASIS + 1, bx + 2, 2, *tile),
            buf(BASIS, bx, *tile),
            buf(BASIS, 2, 2, *tile), buf(BASIS, 2, 2, *tile),
            buf(2, bx // 2, *tile), buf(2, bx // 2, *tile),
            buf(2, bx, LANES), buf(bx, LANES),
            buf(2, bx, LANES), buf(2, bx, LANES),
            buf(2, bx, LANES), buf(4, 2, bx, LANES),
            buf(7, 2, bx, LANES),
            buf(MOMENTS, 5, *tile),
            buf(3, *tile), buf(nx, *tile), buf(nz // 2, *tile), buf(2 * ny, *tile),
            dma((BASIS, 4)), dma((BASIS, 4)), dma((BASIS, 4)), dma((BASIS, 4)),
            dma((2,)), dma((2,)), dma((2,)), dma((2,)), dma((4,)), dma((4,)), dma((4,)), dma((4,)),
            dma((nx,)), dma((nx,)), dma((nz // 2,)), dma((nz // 2,)), dma((2 * ny,)), dma((2 * ny,)),
        ],
        compiler_params=pltpu.CompilerParams(collective_id=0, has_side_effects=True, vmem_limit_bytes=(64 << 20) - 2600000),
    )(charges.reshape(NRHS * bx * by, bz), permittivity.reshape(bx * by, bz), screening.reshape(bx * by, bz))
    columns = NRHS * (BASIS + 1)
    lower = lax.linalg.cholesky(gram[:, :columns], symmetrize_input=False)
    return top.reshape(NRHS, bx, by, bz), lower.T


def solution(mesh):
    sizes = tuple(mesh.shape[a] for a in ("gx", "gy", "gz"))
    placed = (P(None, "gx", "gy", "gz"), P("gx", "gy", "gz"), P("gx", "gy", "gz"))
    return jax.shard_map(
        functools.partial(per_device, sizes),
        mesh=mesh,
        in_specs=placed,
        out_specs=(P(None, "gx", "gy", "gz"), P()),
        check_vma=False,
    )
```

```python
import functools

import jax
import jax.numpy as jnp
from jax import lax
from jax.experimental import pallas as pl
from jax.experimental.pallas import tpu as pltpu
from jax.sharding import PartitionSpec as P

MESH = pl.DeviceIdType.MESH
BASIS = 4
NRHS = 8
LANES = 128
MOMENTS = 2 * BASIS + 1
F32 = jnp.float32


def iota(dim):
    return lax.broadcasted_iota(jnp.int32, (8, LANES), dim)


def kernel(dims, ch_in, eps_in, scr_in, top_out, gram, ch, eps, scr, top, insem, p, ex, ey, eys, wgt, e, inj, yes, yer, sup, rup,
           ce, ie, csend, crecv, ees, eer, wge, acc, sbuf, r1, r2, r3,
           ssem, rsem, xsem, ysem, zsem, tsem, usem, vsem, esem, fsem, gsem, hsem,
           as1, ar1, as2, ar2, as3, ar3):
    bx, by, nx, ny, nz = dims
    ix, iy, iz = (lax.axis_index(a) for a in ("gx", "gy", "gz"))
    zh = lax.rem(iz, 2)
    zx = lax.div(iz, 2)
    lane, row = iota(1), iota(0)
    place = lane & 7
    zero = jnp.zeros((8, LANES), F32)

    faces = (
        (ix < nx - 1, (ix + 1, iy, iz), ix > 0),
        (ix > 0, (ix - 1, iy, iz), ix < nx - 1),
        (iy < ny - 1, (ix, iy + 1, iz), iy > 0),
        (iy > 0, (ix, iy - 1, iz), iy < ny - 1),
        (iz < nz - 1, (ix, iy, iz + 1), iz > 0),
        (iz > 0, (ix, iy, iz - 1), iz < nz - 1),
    )
    n3 = 2 * ny
    me3 = zh * ny + iy

    def peer1(d):
        j = lax.rem(ix + d, nx)
        return j, (j, iy, iz)

    def peer2(d):
        j = lax.rem(zx + d, nz // 2)
        return j, (ix, iy, 2 * j + zh)

    def peer3(d):
        j = lax.rem(me3 + d, n3)
        h = lax.div(j, ny)
        return j, (ix, j - h * ny, 2 * zx + h)

    loads = [pltpu.make_async_copy(src, dst, insem.at[i])
             for i, (src, dst) in enumerate(((ch_in, ch), (eps_in, eps), (scr_in, scr)))]
    for c in loads:
        c.start()

    barrier = pltpu.get_barrier_semaphore()
    count = jnp.int32(0)
    for out, peer, _ in faces[4:]:
        @pl.when(out)
        def _():
            pl.semaphore_signal(barrier, inc=1, device_id=peer, device_id_type=MESH)
        count = count + jnp.where(out, 1, 0)
    for n, peer in ((n3, peer3), (nx, peer1), (nz // 2, peer2)):
        @pl.loop(1, n)
        def _(d):
            pl.semaphore_signal(barrier, inc=1, device_id=peer(d)[1], device_id_type=MESH)
        count = count + (n - 1)

    for c in loads:
        c.wait()

    def inject(y):
        return (lane == (8 * y + 8) % LANES) | (lane == (8 * y - 1) % LANES)

    @pl.loop(0, bx)
    def _(x):
        border, beyond = zero, zero
        for y in range(by):
            v = ch[pl.ds(x * by + y, 8, stride=bx * by), :]
            p[0, x + 1, y + 1] = v
            v = pltpu.roll(v, (8 * y + 4) % LANES, 1)
            border = jnp.where((lane >> 3) == y, v, border)
            beyond = jnp.where(inject(y), v, beyond)
        e[0, x + 1, 0] = border
        e[0, x + 1, 1] = border
        inj[0, x] = beyond
        ex[x + 1] = eps[pl.ds(x * by, by), :]
        ey[x, pl.ds(8, by), :] = eps[pl.ds(x * by, by), :]
        eys[0, pl.ds(x, 1), :] = eps[pl.ds(x * by, 1), :]
        eys[1, pl.ds(x, 1), :] = eps[pl.ds(x * by + by - 1, 1), :]

    @pl.loop(0, bx // 2)
    def _(j):
        even, odd = e[0, 2 * j + 1, 0], e[0, 2 * j + 2, 0]
        sup[0, j] = jnp.where(place < 4, even, pltpu.roll(odd, 4, 1))
        sup[1, j] = jnp.where(place < 4, pltpu.roll(even, LANES - 4, 1), odd)

    lane_e = lax.broadcasted_iota(jnp.int32, (bx, LANES), 1)
    row_e = lax.broadcasted_iota(jnp.int32, (bx, LANES), 0)
    place_e = lane_e & 7
    blank = jnp.zeros((bx, LANES), F32)
    c_e, c_s, i_e = blank, blank, blank
    for y in range(by):
        v = pltpu.roll(eps[pl.ds(y, bx, stride=by), :], (8 * y + 4) % LANES, 1)
        u = pltpu.roll(scr[pl.ds(y, bx, stride=by), :], (8 * y + 4) % LANES, 1)
        c_e = jnp.where((lane_e >> 3) == y, v, c_e)
        c_s = jnp.where((lane_e >> 3) == y, u, c_s)
        i_e = jnp.where((lane_e == (8 * y + 8) % LANES) | (lane_e == (8 * y - 1) % LANES), v, i_e)
    ce[0] = c_e
    ce[1] = c_s
    ie[...] = i_e
    csend[0] = jnp.where(place_e < 4, c_e, pltpu.roll(c_s, 4, 1))
    csend[1] = jnp.where(place_e < 4, pltpu.roll(c_s, LANES - 4, 1), c_e)

    edge = jnp.zeros((by, LANES), F32)
    for there, at, ghost in ((ix == 0, 0, 0), (ix == nx - 1, bx + 1, 1)):
        @pl.when(there)
        def _():
            ex[at] = edge
            for side in range(2):
                eer[ghost, side] = blank

            @pl.loop(0, BASIS)
            def _(k):
                for y in range(by):
                    p[k, at, y + 1] = zero
                e[k, at, 0] = zero
                e[k, at, 1] = zero

    for there, at, ghost in ((iy == 0, 0, 0), (iy == ny - 1, by + 1, 1)):
        @pl.when(there)
        def _():
            ey[pl.ds(bx + ghost, 1)] = jnp.zeros((1, by + 16, LANES), F32)
            for side in range(2):
                eer[2 + ghost, side] = blank

            @pl.loop(0, BASIS)
            def _(k):
                for x in range(bx):
                    p[k, x + 1, at] = zero
                yer[k, ghost, 0] = zero
                yer[k, ghost, 1] = zero

    for there, ghost in ((iz == 0, 0), (iz == nz - 1, 1)):
        @pl.when(there)
        def _():
            crecv[ghost] = blank
            for j in range(bx // 2):
                rup[ghost, j] = zero

    pl.semaphore_wait(barrier, count)

    def remote(src, dst, send, recv, i):
        return pltpu.make_async_remote_copy(
            src_ref=src, dst_ref=dst, send_sem=send, recv_sem=recv, device_id=faces[i][1], device_id_type=MESH)

    def field(k):
        pairs = (
            (p.at[k, bx, pl.ds(1, by)], p.at[k, 0, pl.ds(1, by)]),
            (p.at[k, 1, pl.ds(1, by)], p.at[k, bx + 1, pl.ds(1, by)]),
            (p.at[k, pl.ds(1, bx), by], p.at[k, pl.ds(1, bx), 0]),
            (p.at[k, pl.ds(1, bx), 1], p.at[k, pl.ds(1, bx), by + 1]),
        )
        return [(i, remote(*pairs[i], ssem.at[k, i], rsem.at[k, i], i)) for i in range(4)]

    def rim(k):
        pairs = (
            (e.at[k, bx], e.at[k, 0]),
            (e.at[k, 1], e.at[k, bx + 1]),
            (yes.at[k, 1], yer.at[k, 0]),
            (yes.at[k, 0], yer.at[k, 1]),
        )
        return [(i, remote(*pairs[i], xsem.at[k, i], ysem.at[k, i], i)) for i in range(4)]

    def far():
        return [(4 + i, remote(sup.at[i], rup.at[i], zsem.at[i], tsem.at[i], 4 + i)) for i in range(2)]

    def far_coefficient():
        return [(4 + i, remote(csend.at[i], crecv.at[i], usem.at[i], vsem.at[i], 4 + i)) for i in range(2)]

    def coefficient():
        pairs = (
            (ex.at[bx], ex.at[0]),
            (ex.at[1], ex.at[bx + 1]),
            (eys.at[1], ey.at[bx, pl.ds(8, bx)]),
            (eys.at[0], ey.at[bx + 1, pl.ds(8, bx)]),
        )
        return [(i, remote(*pairs[i], esem.at[i], fsem.at[i], i)) for i in range(4)]

    def rim_coefficient():
        return [(i, remote(ees, eer.at[i], gsem.at[i], hsem.at[i], i)) for i in range(4)]

    def start(copies):
        for i, c in copies:
            @pl.when(faces[i][0])
            def _():
                c.start()

    def arrive(copies):
        for i, c in copies:
            @pl.when(faces[i][2])
            def _():
                c.wait_recv()

    def sent(copies):
        for i, c in copies:
            @pl.when(faces[i][0])
            def _():
                c.wait_send()

    def moments(k):
        inner = (lane >= BASIS) & (lane < LANES - BASIS)

        def body(x, sums):
            sums = list(sums)
            for y in range(by):
                b = p[k, x + 1, y + 1]
                b = jnp.where(inner, b, 0.0)
                for s in range(5):
                    t = b if s == 0 else pltpu.roll(b, s, 0)
                    sums[s] = sums[s] + b * t
                    if k > 0:
                        sums[5 + s] = sums[5 + s] + p[k - 1, x + 1, y + 1] * t
            return tuple(sums)

        sums = lax.fori_loop(0, bx, body, (zero,) * (10 if k else 5))
        for s in range(5):
            acc[2 * k, s] = sums[s]
            if k > 0:
                acc[2 * k - 1, s] = sums[5 + s]

    def rim_moments(k):
        sums = [acc[2 * k, s] for s in range(5)] + ([acc[2 * k - 1, s] for s in range(5)] if k else [])
        for x in range(bx):
            b = jnp.where(place < 4, e[k, x + 1, 1], e[k, x + 1, 0])
            a = jnp.where(place < 4, e[k - 1, x + 1, 1], e[k - 1, x + 1, 0]) if k else None
            for s in range(5):
                t = b if s == 0 else pltpu.roll(b, s, 0)
                sums[s] = sums[s] + b * t
                if k > 0:
                    sums[5 + s] = sums[5 + s] + a * t
        for s in range(5):
            acc[2 * k, s] = sums[s]
            if k > 0:
                acc[2 * k - 1, s] = sums[5 + s]

    def reduce(first, last, table):
        for m in range(first, last):
            for s in range(8):
                part = acc[m, s] if s <= 4 else pltpu.roll(acc[m, 8 - s], s, 0)
                col = jnp.sum(part, axis=1, keepdims=True)
                table = jnp.where(lane == 8 * m + ((row - s) & 7), col, table)
        return table

    def spread(ref, *at):
        return jnp.broadcast_to(ref[at], (8, LANES))

    def cells(k, x, ys, beyond):
        for y in ys:
            v = p[k, x + 1, y + 1]
            near = (p[k, x, y + 1], p[k, x + 2, y + 1], p[k, x + 1, y], p[k, x + 1, y + 2],
                    pltpu.roll(v, 1, 1), pltpu.roll(v, LANES - 1, 1))
            w = [spread(wgt, i, x, pl.ds(y, 1)) for i in range(7)]
            t = [w[i] * near[i] for i in range(6)]
            v = w[6] * v - (((t[0] + t[1]) + (t[2] + t[3])) + (t[4] + t[5]))
            p[k + 1, x + 1, y + 1] = v
            if k < BASIS - 1:
                beyond = jnp.where(inject(y), pltpu.roll(v, (8 * y + 4) % LANES, 1), beyond)
        if k < BASIS - 1:
            inj[k + 1, x] = beyond

    def interior(k):
        @pl.loop(1, bx - 1)
        def _(x):
            cells(k, x, range(1, by - 1), zero)

    def border(k):
        @pl.loop(0, 2)
        def _(j):
            cells(k, j * (bx - 1), range(by), zero)

        @pl.loop(0, 2)
        def _(j):
            for i in range(bx // 2 - 1):
                x = 1 + j * (bx // 2 - 1) + i
                cells(k, x, (0, by - 1), inj[k + 1, x] if k < BASIS - 1 else zero)

    def rim_edges(k):
        for side in range(2):
            low, high = zero, zero
            for x in range(bx):
                v = e[k, x + 1, side]
                here = (lane >> 3) == x
                low = jnp.where(here, pltpu.roll(v, 8 * x, 1) if x else v, low)
                high = jnp.where(here, pltpu.roll(v, (8 * x + 8) % LANES, 1), high)
            yes[k, 0, side] = low
            yes[k, 1, side] = high

    def rim_step(k):
        for side in range(2):
            before, after = yer[k, 0, side], yer[k, 1, side]
            low, high = zero, zero
            for x in range(bx):
                v = e[k, x + 1, side]
                beyond = inj[k, x]
                ym = jnp.where(lane < 8, pltpu.roll(before, (LANES - 8 * x) % LANES, 1), pltpu.roll(v, 8, 1))
                yp = jnp.where(lane >= LANES - 8, pltpu.roll(after, LANES - 8 - 8 * x, 1), pltpu.roll(v, LANES - 8, 1))
                zm = pltpu.roll(jnp.where(place == 7, beyond, v) if side else v, 1, 1)
                zp = pltpu.roll(v if side else jnp.where(place == 0, beyond, v), LANES - 1, 1)
                near = (e[k, x, side], e[k, x + 2, side], ym, yp, zm, zp)
                w = [spread(wge, i, side, pl.ds(x, 1)) for i in range(7)]
                t = [w[i] * near[i] for i in range(6)]
                v = w[6] * v - (((t[0] + t[1]) + (t[2] + t[3])) + (t[4] + t[5]))
                e[k + 1, x + 1, side] = v
                if k < BASIS - 1:
                    here = (lane >> 3) == x
                    low = jnp.where(here, pltpu.roll(v, 8 * x, 1) if x else v, low)
                    high = jnp.where(here, pltpu.roll(v, (8 * x + 8) % LANES, 1), high)
            if k < BASIS - 1:
                yes[k + 1, 0, side] = low
                yes[k + 1, 1, side] = high

    start(coefficient())
    start(field(0))
    start(far())
    start(far_coefficient())
    moments(0)

    arrive(coefficient())

    @pl.loop(0, bx)
    def _(x):
        c = eps[pl.ds(x * by, by), :]
        ey[x, pl.ds(0, 8), :] = spread(ey, bx, pl.ds(8 + x, 1))
        ey[x, pl.ds(8 + by, 8), :] = spread(ey, bx + 1, pl.ds(8 + x, 1))
        total = scr[pl.ds(x * by, by), :] * 0.02 - 0.4
        near = (ex[x], ex[x + 2], ey[x, pl.ds(7, by), :], ey[x, pl.ds(9, by), :],
                pltpu.roll(c, 1, 1), pltpu.roll(c, LANES - 1, 1))
        for i, n in enumerate(near):
            w = (c + n) * 0.01
            wgt[i, x] = w
            total = total + w
        wgt[6, x] = total

    interior(0)
    arrive(field(0))
    border(0)
    start(field(1))
    interior(1)
    moments(1)
    arrive(field(1))
    border(1)
    start(field(2))
    interior(2)

    arrive(far())
    arrive(far_coefficient())

    @pl.loop(0, bx // 2)
    def _(j):
        even, odd = e[0, 2 * j + 1, 0], e[0, 2 * j + 2, 0]
        lo, hi = rup[0, j], rup[1, j]
        e[0, 2 * j + 1, 0] = jnp.where(place < 4, lo, even)
        e[0, 2 * j + 2, 0] = jnp.where(place < 4, pltpu.roll(lo, LANES - 4, 1), odd)
        e[0, 2 * j + 1, 1] = jnp.where(place < 4, even, pltpu.roll(hi, 4, 1))
        e[0, 2 * j + 2, 1] = jnp.where(place < 4, odd, hi)

    rim_edges(0)
    c_e, c_s = ce[0], ce[1]
    e_side = (jnp.where(place_e < 4, crecv[0], c_e), jnp.where(place_e < 4, c_e, crecv[1]))
    s_side = (jnp.where(place_e < 4, pltpu.roll(crecv[0], LANES - 4, 1), c_s),
              jnp.where(place_e < 4, c_s, pltpu.roll(crecv[1], 4, 1)))
    ees[0] = e_side[0]
    ees[1] = e_side[1]
    start(rim_coefficient())
    start(rim(0))
    moments(2)

    arrive(rim_coefficient())
    for side in range(2):
        c, beyond = ees[side], ie[...]
        xm = jnp.where(row_e == 0, pltpu.roll(eer[0, side], 1, 0), pltpu.roll(c, 1, 0))
        xp = jnp.where(row_e == bx - 1, pltpu.roll(eer[1, side], bx - 1, 0), pltpu.roll(c, bx - 1, 0))
        ym = jnp.where(lane_e < 8, pltpu.roll(eer[2, side], 8, 1), pltpu.roll(c, 8, 1))
        yp = jnp.where(lane_e >= LANES - 8, pltpu.roll(eer[3, side], LANES - 8, 1), pltpu.roll(c, LANES - 8, 1))
        zm = pltpu.roll(jnp.where(place_e == 7, beyond, c) if side else c, 1, 1)
        zp = pltpu.roll(c if side else jnp.where(place_e == 0, beyond, c), LANES - 1, 1)
        if side:
            inside = (place_e < 4) | (iz < nz - 1)
        else:
            inside = (place_e >= 4) | (iz > 0)
        total = s_side[side] * 0.02 - 0.4
        for i, n in enumerate((xm, xp, ym, yp, zm, zp)):
            w = (c + n) * 0.01
            wge[i, side] = jnp.where(inside, w, 0.0)
            total = total + w
        wge[6, side] = jnp.where(inside, total, 0.0)

    arrive(rim(0))
    rim_step(0)
    start(rim(1))
    arrive(field(2))
    border(2)
    start(field(3))
    arrive(rim(1))
    rim_step(1)
    start(rim(2))
    interior(3)
    moments(3)
    arrive(rim(2))
    rim_step(2)
    start(rim(3))
    arrive(field(3))
    border(3)
    moments(4)
    for k in range(BASIS):
        rim_moments(k)
    table = reduce(0, 2 * BASIS - 1, zero)
    arrive(rim(3))
    rim_step(3)
    rim_moments(BASIS)
    total = reduce(2 * BASIS - 1, MOMENTS, table)

    store = pltpu.make_async_copy(top, top_out, insem.at[3])
    for stage, (n, peer, me, slots, send, recv) in enumerate((
        (nx, peer1, ix, r1, as1, ar1), (nz // 2, peer2, zx, r2, as2, ar2), (n3, peer3, me3, r3, as3, ar3))):
        sbuf[stage] = total
        slots[me] = total

        def copy(d, mine):
            j, device = peer(d)
            return pltpu.make_async_remote_copy(
                src_ref=sbuf.at[stage], dst_ref=slots.at[me if mine else j], send_sem=send.at[d],
                recv_sem=recv.at[me if mine else j], device_id=device, device_id_type=MESH)

        @pl.loop(1, n)
        def _(d):
            copy(d, True).start()

        if stage == 0:
            for k in range(BASIS):
                sent(field(k))
                sent(rim(k))
            for c in (far(), far_coefficient(), coefficient(), rim_coefficient()):
                sent(c)

        if stage == 2:
            @pl.loop(0, bx)
            def _(x):
                border = jnp.where(place < 4, e[BASIS, x + 1, 1], e[BASIS, x + 1, 0])
                inner = (lane >= BASIS) & (lane < LANES - BASIS)
                for y in range(by):
                    v = jnp.where(inner, p[BASIS, x + 1, y + 1], pltpu.roll(border, (LANES - 4 - 8 * y) % LANES, 1))
                    top[pl.ds(x * by + y, 8, stride=bx * by), :] = v
            store.start()

        @pl.loop(1, n)
        def _(d):
            copy(d, False).wait_recv()
        parts = [slots[j] for j in range(n)]
        while len(parts) > 1:
            parts = [parts[i] + parts[i + 1] for i in range(0, len(parts) - 1, 2)] + ([parts[-1]] if len(parts) % 2 else [])
        total = parts[0]

        @pl.loop(1, n)
        def _(d):
            copy(d, True).wait_send()

    store.wait()
    cells = bx * by * LANES * nx * ny * nz
    total = total * (1.0 / cells)
    for i in range(BASIS + 1):
        gram[pl.ds(8 * i, 8), :] = total if i == 0 else pltpu.roll(total, LANES - 8 * i, 1)


def per_device(sizes, charges, permittivity, screening):
    _, bx, by, bz = charges.shape
    nx, ny, nz = sizes
    dims = (bx, by, nx, ny, nz)
    vmem = pl.BlockSpec(memory_space=pltpu.VMEM)
    dma = pltpu.SemaphoreType.DMA

    def buf(*shape):
        return pltpu.VMEM(shape, F32)

    tile = (8, LANES)
    top, gram = pl.pallas_call(
        functools.partial(kernel, dims),
        out_shape=(
            jax.ShapeDtypeStruct((NRHS * bx * by, bz), F32),
            jax.ShapeDtypeStruct((8 * (BASIS + 1), LANES), F32),
        ),
        in_specs=[pl.BlockSpec(memory_space=pltpu.HBM)] * 3,
        out_specs=(pl.BlockSpec(memory_space=pltpu.HBM), vmem),
        scratch_shapes=[
            buf(NRHS * bx * by, LANES), buf(bx * by, LANES), buf(bx * by, LANES),
            buf(NRHS * bx * by, LANES),
            dma((4,)),
            buf(BASIS + 1, bx + 2, by + 2, *tile),
            buf(bx + 2, by, LANES),
            buf(bx + 2, by + 16, LANES),
            buf(2, bx, LANES),
            buf(7, bx, by, LANES),
            buf(BASIS + 1, bx + 2, 2, *tile),
            buf(BASIS, bx, *tile),
            buf(BASIS, 2, 2, *tile), buf(BASIS, 2, 2, *tile),
            buf(2, bx // 2, *tile), buf(2, bx // 2, *tile),
            buf(2, bx, LANES), buf(bx, LANES),
            buf(2, bx, LANES), buf(2, bx, LANES),
            buf(2, bx, LANES), buf(4, 2, bx, LANES),
            buf(7, 2, bx, LANES),
            buf(MOMENTS, 5, *tile),
            buf(3, *tile), buf(nx, *tile), buf(nz // 2, *tile), buf(2 * ny, *tile),
            dma((BASIS, 4)), dma((BASIS, 4)), dma((BASIS, 4)), dma((BASIS, 4)),
            dma((2,)), dma((2,)), dma((2,)), dma((2,)), dma((4,)), dma((4,)), dma((4,)), dma((4,)),
            dma((nx,)), dma((nx,)), dma((nz // 2,)), dma((nz // 2,)), dma((2 * ny,)), dma((2 * ny,)),
        ],
        compiler_params=pltpu.CompilerParams(collective_id=0, has_side_effects=True, vmem_limit_bytes=(64 << 20) - 9000000),
    )(charges.reshape(NRHS * bx * by, bz), permittivity.reshape(bx * by, bz), screening.reshape(bx * by, bz))
    columns = NRHS * (BASIS + 1)
    lower = lax.linalg.cholesky(gram[:, :columns], symmetrize_input=False)
    top, r_factor = pl.pallas_call(
        finish,
        out_shape=(
            jax.ShapeDtypeStruct((NRHS * bx * by, bz), F32),
            jax.ShapeDtypeStruct((columns, columns), F32),
        ),
        in_specs=[vmem] * 2,
        out_specs=(vmem, vmem),
        compiler_params=pltpu.CompilerParams(vmem_limit_bytes=8 << 20),
    )(top, lower)
    return top.reshape(NRHS, bx, by, bz), r_factor


def finish(top_in, lower, top, r_factor):
    top[...] = top_in[...]
    r_factor[...] = lower[...].T


def solution(mesh):
    sizes = tuple(mesh.shape[a] for a in ("gx", "gy", "gz"))
    placed = (P(None, "gx", "gy", "gz"), P("gx", "gy", "gz"), P("gx", "gy", "gz"))
    return jax.shard_map(
        functools.partial(per_device, sizes),
        mesh=mesh,
        in_specs=placed,
        out_specs=(P(None, "gx", "gy", "gz"), P()),
        check_vma=False,
    )
```

```python
import functools

import jax
import jax.numpy as jnp
from jax import lax
from jax.experimental import pallas as pl
from jax.experimental.pallas import tpu as pltpu
from jax.sharding import PartitionSpec as P

MESH = pl.DeviceIdType.MESH
BASIS = 4
NRHS = 8
LANES = 128
MOMENTS = 2 * BASIS + 1
F32 = jnp.float32


def iota(dim):
    return lax.broadcasted_iota(jnp.int32, (8, LANES), dim)


def kernel(dims, ch_in, eps_in, scr_in, top_out, gram, ch, eps, scr, top, insem, p, ex, ey, eys, wgt, e, inj, yes, yer, sup, rup,
           ce, ie, csend, crecv, ees, eer, wge, acc, sbuf, r1, r2, r3,
           ssem, rsem, xsem, ysem, zsem, tsem, usem, vsem, esem, fsem, gsem, hsem,
           as1, ar1, as2, ar2, as3, ar3):
    bx, by, nx, ny, nz = dims
    ix, iy, iz = (lax.axis_index(a) for a in ("gx", "gy", "gz"))
    zh = lax.rem(iz, 2)
    zx = lax.div(iz, 2)
    lane, row = iota(1), iota(0)
    place = lane & 7
    zero = jnp.zeros((8, LANES), F32)

    faces = (
        (ix < nx - 1, (ix + 1, iy, iz), ix > 0),
        (ix > 0, (ix - 1, iy, iz), ix < nx - 1),
        (iy < ny - 1, (ix, iy + 1, iz), iy > 0),
        (iy > 0, (ix, iy - 1, iz), iy < ny - 1),
        (iz < nz - 1, (ix, iy, iz + 1), iz > 0),
        (iz > 0, (ix, iy, iz - 1), iz < nz - 1),
    )
    n3 = 2 * ny
    me3 = zh * ny + iy

    def peer1(d):
        j = lax.rem(ix + d, nx)
        return j, (j, iy, iz)

    def peer2(d):
        j = lax.rem(zx + d, nz // 2)
        return j, (ix, iy, 2 * j + zh)

    def peer3(d):
        j = lax.rem(me3 + d, n3)
        h = lax.div(j, ny)
        return j, (ix, j - h * ny, 2 * zx + h)

    loads = [pltpu.make_async_copy(src, dst, insem.at[i])
             for i, (src, dst) in enumerate(((ch_in, ch), (eps_in, eps), (scr_in, scr)))]
    for c in loads:
        c.start()

    barrier = pltpu.get_barrier_semaphore()
    count = jnp.int32(0)
    for out, peer, _ in faces[4:]:
        @pl.when(out)
        def _():
            pl.semaphore_signal(barrier, inc=1, device_id=peer, device_id_type=MESH)
        count = count + jnp.where(out, 1, 0)
    for n, peer in ((n3, peer3), (nx, peer1), (nz // 2, peer2)):
        @pl.loop(1, n)
        def _(d):
            pl.semaphore_signal(barrier, inc=1, device_id=peer(d)[1], device_id_type=MESH)
        count = count + (n - 1)

    for c in loads:
        c.wait()

    def inject(y):
        return (lane == (8 * y + 8) % LANES) | (lane == (8 * y - 1) % LANES)

    @pl.loop(0, bx)
    def _(x):
        border, beyond = zero, zero
        for y in range(by):
            v = ch[pl.ds(x * by + y, 8, stride=bx * by), :]
            p[0, x + 1, y + 1] = v
            v = pltpu.roll(v, (8 * y + 4) % LANES, 1)
            border = jnp.where((lane >> 3) == y, v, border)
            beyond = jnp.where(inject(y), v, beyond)
        e[0, x + 1, 0] = border
        e[0, x + 1, 1] = border
        inj[0, x] = beyond
        ex[x + 1] = eps[pl.ds(x * by, by), :]
        ey[x, pl.ds(8, by), :] = eps[pl.ds(x * by, by), :]
        eys[0, pl.ds(x, 1), :] = eps[pl.ds(x * by, 1), :]
        eys[1, pl.ds(x, 1), :] = eps[pl.ds(x * by + by - 1, 1), :]

    @pl.loop(0, bx // 2)
    def _(j):
        even, odd = e[0, 2 * j + 1, 0], e[0, 2 * j + 2, 0]
        sup[0, j] = jnp.where(place < 4, even, pltpu.roll(odd, 4, 1))
        sup[1, j] = jnp.where(place < 4, pltpu.roll(even, LANES - 4, 1), odd)

    lane_e = lax.broadcasted_iota(jnp.int32, (bx, LANES), 1)
    row_e = lax.broadcasted_iota(jnp.int32, (bx, LANES), 0)
    place_e = lane_e & 7
    blank = jnp.zeros((bx, LANES), F32)
    c_e, c_s, i_e = blank, blank, blank
    for y in range(by):
        v = pltpu.roll(eps[pl.ds(y, bx, stride=by), :], (8 * y + 4) % LANES, 1)
        u = pltpu.roll(scr[pl.ds(y, bx, stride=by), :], (8 * y + 4) % LANES, 1)
        c_e = jnp.where((lane_e >> 3) == y, v, c_e)
        c_s = jnp.where((lane_e >> 3) == y, u, c_s)
        i_e = jnp.where((lane_e == (8 * y + 8) % LANES) | (lane_e == (8 * y - 1) % LANES), v, i_e)
    ce[0] = c_e
    ce[1] = c_s
    ie[...] = i_e
    csend[0] = jnp.where(place_e < 4, c_e, pltpu.roll(c_s, 4, 1))
    csend[1] = jnp.where(place_e < 4, pltpu.roll(c_s, LANES - 4, 1), c_e)

    edge = jnp.zeros((by, LANES), F32)
    for there, at, ghost in ((ix == 0, 0, 0), (ix == nx - 1, bx + 1, 1)):
        @pl.when(there)
        def _():
            ex[at] = edge
            for side in range(2):
                eer[ghost, side] = blank

            @pl.loop(0, BASIS)
            def _(k):
                for y in range(by):
                    p[k, at, y + 1] = zero
                e[k, at, 0] = zero
                e[k, at, 1] = zero

    for there, at, ghost in ((iy == 0, 0, 0), (iy == ny - 1, by + 1, 1)):
        @pl.when(there)
        def _():
            ey[pl.ds(bx + ghost, 1)] = jnp.zeros((1, by + 16, LANES), F32)
            for side in range(2):
                eer[2 + ghost, side] = blank

            @pl.loop(0, BASIS)
            def _(k):
                for x in range(bx):
                    p[k, x + 1, at] = zero
                yer[k, ghost, 0] = zero
                yer[k, ghost, 1] = zero

    for there, ghost in ((iz == 0, 0), (iz == nz - 1, 1)):
        @pl.when(there)
        def _():
            crecv[ghost] = blank
            for j in range(bx // 2):
                rup[ghost, j] = zero

    pl.semaphore_wait(barrier, count)

    def remote(src, dst, send, recv, i):
        return pltpu.make_async_remote_copy(
            src_ref=src, dst_ref=dst, send_sem=send, recv_sem=recv, device_id=faces[i][1], device_id_type=MESH)

    def field(k):
        pairs = (
            (p.at[k, bx, pl.ds(1, by)], p.at[k, 0, pl.ds(1, by)]),
            (p.at[k, 1, pl.ds(1, by)], p.at[k, bx + 1, pl.ds(1, by)]),
            (p.at[k, pl.ds(1, bx), by], p.at[k, pl.ds(1, bx), 0]),
            (p.at[k, pl.ds(1, bx), 1], p.at[k, pl.ds(1, bx), by + 1]),
        )
        return [(i, remote(*pairs[i], ssem.at[k, i], rsem.at[k, i], i)) for i in range(4)]

    def rim(k):
        pairs = (
            (e.at[k, bx], e.at[k, 0]),
            (e.at[k, 1], e.at[k, bx + 1]),
            (yes.at[k, 1], yer.at[k, 0]),
            (yes.at[k, 0], yer.at[k, 1]),
        )
        return [(i, remote(*pairs[i], xsem.at[k, i], ysem.at[k, i], i)) for i in range(4)]

    def far():
        return [(4 + i, remote(sup.at[i], rup.at[i], zsem.at[i], tsem.at[i], 4 + i)) for i in range(2)]

    def far_coefficient():
        return [(4 + i, remote(csend.at[i], crecv.at[i], usem.at[i], vsem.at[i], 4 + i)) for i in range(2)]

    def coefficient():
        pairs = (
            (ex.at[bx], ex.at[0]),
            (ex.at[1], ex.at[bx + 1]),
            (eys.at[1], ey.at[bx, pl.ds(8, bx)]),
            (eys.at[0], ey.at[bx + 1, pl.ds(8, bx)]),
        )
        return [(i, remote(*pairs[i], esem.at[i], fsem.at[i], i)) for i in range(4)]

    def rim_coefficient():
        return [(i, remote(ees, eer.at[i], gsem.at[i], hsem.at[i], i)) for i in range(4)]

    def start(copies):
        for i, c in copies:
            @pl.when(faces[i][0])
            def _():
                c.start()

    def arrive(copies):
        for i, c in copies:
            @pl.when(faces[i][2])
            def _():
                c.wait_recv()

    def sent(copies):
        for i, c in copies:
            @pl.when(faces[i][0])
            def _():
                c.wait_send()

    def moments(k):
        inner = (lane >= BASIS) & (lane < LANES - BASIS)

        def body(x, sums):
            sums = list(sums)
            for y in range(by):
                b = p[k, x + 1, y + 1]
                b = jnp.where(inner, b, 0.0)
                for s in range(5):
                    t = b if s == 0 else pltpu.roll(b, s, 0)
                    sums[s] = sums[s] + b * t
                    if k > 0:
                        sums[5 + s] = sums[5 + s] + p[k - 1, x + 1, y + 1] * t
            return tuple(sums)

        sums = lax.fori_loop(0, bx, body, (zero,) * (10 if k else 5))
        for s in range(5):
            acc[2 * k, s] = sums[s]
            if k > 0:
                acc[2 * k - 1, s] = sums[5 + s]

    def rim_moments(k):
        sums = [acc[2 * k, s] for s in range(5)] + ([acc[2 * k - 1, s] for s in range(5)] if k else [])
        for x in range(bx):
            b = jnp.where(place < 4, e[k, x + 1, 1], e[k, x + 1, 0])
            a = jnp.where(place < 4, e[k - 1, x + 1, 1], e[k - 1, x + 1, 0]) if k else None
            for s in range(5):
                t = b if s == 0 else pltpu.roll(b, s, 0)
                sums[s] = sums[s] + b * t
                if k > 0:
                    sums[5 + s] = sums[5 + s] + a * t
        for s in range(5):
            acc[2 * k, s] = sums[s]
            if k > 0:
                acc[2 * k - 1, s] = sums[5 + s]

    def reduce(first, last, table):
        for m in range(first, last):
            for s in range(8):
                part = acc[m, s] if s <= 4 else pltpu.roll(acc[m, 8 - s], s, 0)
                col = jnp.sum(part, axis=1, keepdims=True)
                table = jnp.where(lane == 8 * m + ((row - s) & 7), col, table)
        return table

    def spread(ref, *at):
        return jnp.broadcast_to(ref[at], (8, LANES))

    def cells(k, x, ys, beyond):
        for y in ys:
            v = p[k, x + 1, y + 1]
            near = (p[k, x, y + 1], p[k, x + 2, y + 1], p[k, x + 1, y], p[k, x + 1, y + 2],
                    pltpu.roll(v, 1, 1), pltpu.roll(v, LANES - 1, 1))
            w = [spread(wgt, i, x, pl.ds(y, 1)) for i in range(7)]
            t = [w[i] * near[i] for i in range(6)]
            v = w[6] * v - (((t[0] + t[1]) + (t[2] + t[3])) + (t[4] + t[5]))
            p[k + 1, x + 1, y + 1] = v
            if k < BASIS - 1:
                beyond = jnp.where(inject(y), pltpu.roll(v, (8 * y + 4) % LANES, 1), beyond)
        if k < BASIS - 1:
            inj[k + 1, x] = beyond

    def interior(k):
        @pl.loop(1, bx - 1)
        def _(x):
            cells(k, x, range(1, by - 1), zero)

    def border(k):
        @pl.loop(0, 2)
        def _(j):
            cells(k, j * (bx - 1), range(by), zero)

        @pl.loop(0, 2)
        def _(j):
            for i in range(bx // 2 - 1):
                x = 1 + j * (bx // 2 - 1) + i
                cells(k, x, (0, by - 1), inj[k + 1, x] if k < BASIS - 1 else zero)

    def rim_edges(k):
        for side in range(2):
            low, high = zero, zero
            for x in range(bx):
                v = e[k, x + 1, side]
                here = (lane >> 3) == x
                low = jnp.where(here, pltpu.roll(v, 8 * x, 1) if x else v, low)
                high = jnp.where(here, pltpu.roll(v, (8 * x + 8) % LANES, 1), high)
            yes[k, 0, side] = low
            yes[k, 1, side] = high

    def rim_step(k):
        for side in range(2):
            before, after = yer[k, 0, side], yer[k, 1, side]
            low, high = zero, zero
            for x in range(bx):
                v = e[k, x + 1, side]
                beyond = inj[k, x]
                ym = jnp.where(lane < 8, pltpu.roll(before, (LANES - 8 * x) % LANES, 1), pltpu.roll(v, 8, 1))
                yp = jnp.where(lane >= LANES - 8, pltpu.roll(after, LANES - 8 - 8 * x, 1), pltpu.roll(v, LANES - 8, 1))
                zm = pltpu.roll(jnp.where(place == 7, beyond, v) if side else v, 1, 1)
                zp = pltpu.roll(v if side else jnp.where(place == 0, beyond, v), LANES - 1, 1)
                near = (e[k, x, side], e[k, x + 2, side], ym, yp, zm, zp)
                w = [spread(wge, i, side, pl.ds(x, 1)) for i in range(7)]
                t = [w[i] * near[i] for i in range(6)]
                v = w[6] * v - (((t[0] + t[1]) + (t[2] + t[3])) + (t[4] + t[5]))
                e[k + 1, x + 1, side] = v
                if k < BASIS - 1:
                    here = (lane >> 3) == x
                    low = jnp.where(here, pltpu.roll(v, 8 * x, 1) if x else v, low)
                    high = jnp.where(here, pltpu.roll(v, (8 * x + 8) % LANES, 1), high)
            if k < BASIS - 1:
                yes[k + 1, 0, side] = low
                yes[k + 1, 1, side] = high

    start(coefficient())
    start(field(0))
    start(far())
    start(far_coefficient())
    moments(0)

    arrive(coefficient())

    @pl.loop(0, bx)
    def _(x):
        c = eps[pl.ds(x * by, by), :]
        ey[x, pl.ds(0, 8), :] = spread(ey, bx, pl.ds(8 + x, 1))
        ey[x, pl.ds(8 + by, 8), :] = spread(ey, bx + 1, pl.ds(8 + x, 1))
        total = scr[pl.ds(x * by, by), :] * 0.02 - 0.4
        near = (ex[x], ex[x + 2], ey[x, pl.ds(7, by), :], ey[x, pl.ds(9, by), :],
                pltpu.roll(c, 1, 1), pltpu.roll(c, LANES - 1, 1))
        for i, n in enumerate(near):
            w = (c + n) * 0.01
            wgt[i, x] = w
            total = total + w
        wgt[6, x] = total

    interior(0)
    arrive(field(0))
    border(0)
    start(field(1))
    interior(1)
    moments(1)
    arrive(field(1))
    border(1)
    start(field(2))
    interior(2)

    arrive(far())
    arrive(far_coefficient())

    @pl.loop(0, bx // 2)
    def _(j):
        even, odd = e[0, 2 * j + 1, 0], e[0, 2 * j + 2, 0]
        lo, hi = rup[0, j], rup[1, j]
        e[0, 2 * j + 1, 0] = jnp.where(place < 4, lo, even)
        e[0, 2 * j + 2, 0] = jnp.where(place < 4, pltpu.roll(lo, LANES - 4, 1), odd)
        e[0, 2 * j + 1, 1] = jnp.where(place < 4, even, pltpu.roll(hi, 4, 1))
        e[0, 2 * j + 2, 1] = jnp.where(place < 4, odd, hi)

    rim_edges(0)
    c_e, c_s = ce[0], ce[1]
    e_side = (jnp.where(place_e < 4, crecv[0], c_e), jnp.where(place_e < 4, c_e, crecv[1]))
    s_side = (jnp.where(place_e < 4, pltpu.roll(crecv[0], LANES - 4, 1), c_s),
              jnp.where(place_e < 4, c_s, pltpu.roll(crecv[1], 4, 1)))
    ees[0] = e_side[0]
    ees[1] = e_side[1]
    start(rim_coefficient())
    start(rim(0))

    arrive(field(2))
    border(2)
    start(field(3))
    arrive(rim_coefficient())
    for side in range(2):
        c, beyond = ees[side], ie[...]
        xm = jnp.where(row_e == 0, pltpu.roll(eer[0, side], 1, 0), pltpu.roll(c, 1, 0))
        xp = jnp.where(row_e == bx - 1, pltpu.roll(eer[1, side], bx - 1, 0), pltpu.roll(c, bx - 1, 0))
        ym = jnp.where(lane_e < 8, pltpu.roll(eer[2, side], 8, 1), pltpu.roll(c, 8, 1))
        yp = jnp.where(lane_e >= LANES - 8, pltpu.roll(eer[3, side], LANES - 8, 1), pltpu.roll(c, LANES - 8, 1))
        zm = pltpu.roll(jnp.where(place_e == 7, beyond, c) if side else c, 1, 1)
        zp = pltpu.roll(c if side else jnp.where(place_e == 0, beyond, c), LANES - 1, 1)
        if side:
            inside = (place_e < 4) | (iz < nz - 1)
        else:
            inside = (place_e >= 4) | (iz > 0)
        total = s_side[side] * 0.02 - 0.4
        for i, n in enumerate((xm, xp, ym, yp, zm, zp)):
            w = (c + n) * 0.01
            wge[i, side] = jnp.where(inside, w, 0.0)
            total = total + w
        wge[6, side] = jnp.where(inside, total, 0.0)

    arrive(rim(0))
    rim_step(0)
    start(rim(1))
    moments(2)
    arrive(rim(1))
    rim_step(1)
    start(rim(2))
    interior(3)
    moments(3)
    arrive(rim(2))
    rim_step(2)
    start(rim(3))
    arrive(field(3))
    border(3)
    moments(4)
    for k in range(BASIS):
        rim_moments(k)
    table = reduce(0, 2 * BASIS - 1, zero)
    arrive(rim(3))
    rim_step(3)
    rim_moments(BASIS)
    total = reduce(2 * BASIS - 1, MOMENTS, table)

    store = pltpu.make_async_copy(top, top_out, insem.at[3])
    for stage, (n, peer, me, slots, send, recv) in enumerate((
        (nx, peer1, ix, r1, as1, ar1), (nz // 2, peer2, zx, r2, as2, ar2), (n3, peer3, me3, r3, as3, ar3))):
        sbuf[stage] = total
        slots[me] = total

        def copy(d, mine):
            j, device = peer(d)
            return pltpu.make_async_remote_copy(
                src_ref=sbuf.at[stage], dst_ref=slots.at[me if mine else j], send_sem=send.at[d],
                recv_sem=recv.at[me if mine else j], device_id=device, device_id_type=MESH)

        @pl.loop(1, n)
        def _(d):
            copy(d, True).start()

        if stage == 0:
            for k in range(BASIS):
                sent(field(k))
                sent(rim(k))
            for c in (far(), far_coefficient(), coefficient(), rim_coefficient()):
                sent(c)

        if stage == 2:
            @pl.loop(0, bx)
            def _(x):
                border = jnp.where(place < 4, e[BASIS, x + 1, 1], e[BASIS, x + 1, 0])
                inner = (lane >= BASIS) & (lane < LANES - BASIS)
                for y in range(by):
                    v = jnp.where(inner, p[BASIS, x + 1, y + 1], pltpu.roll(border, (LANES - 4 - 8 * y) % LANES, 1))
                    top[pl.ds(x * by + y, 8, stride=bx * by), :] = v
            store.start()

        @pl.loop(1, n)
        def _(d):
            copy(d, False).wait_recv()
        parts = [slots[j] for j in range(n)]
        while len(parts) > 1:
            parts = [parts[i] + parts[i + 1] for i in range(0, len(parts) - 1, 2)] + ([parts[-1]] if len(parts) % 2 else [])
        total = parts[0]

        @pl.loop(1, n)
        def _(d):
            copy(d, True).wait_send()

    store.wait()
    cells = bx * by * LANES * nx * ny * nz
    total = total * (1.0 / cells)
    for i in range(BASIS + 1):
        gram[pl.ds(8 * i, 8), :] = total if i == 0 else pltpu.roll(total, LANES - 8 * i, 1)


def per_device(sizes, charges, permittivity, screening):
    _, bx, by, bz = charges.shape
    nx, ny, nz = sizes
    dims = (bx, by, nx, ny, nz)
    vmem = pl.BlockSpec(memory_space=pltpu.VMEM)
    dma = pltpu.SemaphoreType.DMA

    def buf(*shape):
        return pltpu.VMEM(shape, F32)

    tile = (8, LANES)
    top, gram = pl.pallas_call(
        functools.partial(kernel, dims),
        out_shape=(
            jax.ShapeDtypeStruct((NRHS * bx * by, bz), F32),
            jax.ShapeDtypeStruct((8 * (BASIS + 1), LANES), F32),
        ),
        in_specs=[pl.BlockSpec(memory_space=pltpu.HBM)] * 3,
        out_specs=(pl.BlockSpec(memory_space=pltpu.HBM), vmem),
        scratch_shapes=[
            buf(NRHS * bx * by, LANES), buf(bx * by, LANES), buf(bx * by, LANES),
            buf(NRHS * bx * by, LANES),
            dma((4,)),
            buf(BASIS + 1, bx + 2, by + 2, *tile),
            buf(bx + 2, by, LANES),
            buf(bx + 2, by + 16, LANES),
            buf(2, bx, LANES),
            buf(7, bx, by, LANES),
            buf(BASIS + 1, bx + 2, 2, *tile),
            buf(BASIS, bx, *tile),
            buf(BASIS, 2, 2, *tile), buf(BASIS, 2, 2, *tile),
            buf(2, bx // 2, *tile), buf(2, bx // 2, *tile),
            buf(2, bx, LANES), buf(bx, LANES),
            buf(2, bx, LANES), buf(2, bx, LANES),
            buf(2, bx, LANES), buf(4, 2, bx, LANES),
            buf(7, 2, bx, LANES),
            buf(MOMENTS, 5, *tile),
            buf(3, *tile), buf(nx, *tile), buf(nz // 2, *tile), buf(2 * ny, *tile),
            dma((BASIS, 4)), dma((BASIS, 4)), dma((BASIS, 4)), dma((BASIS, 4)),
            dma((2,)), dma((2,)), dma((2,)), dma((2,)), dma((4,)), dma((4,)), dma((4,)), dma((4,)),
            dma((nx,)), dma((nx,)), dma((nz // 2,)), dma((nz // 2,)), dma((2 * ny,)), dma((2 * ny,)),
        ],
        compiler_params=pltpu.CompilerParams(collective_id=0, has_side_effects=True, vmem_limit_bytes=(64 << 20) - 9000000),
    )(charges.reshape(NRHS * bx * by, bz), permittivity.reshape(bx * by, bz), screening.reshape(bx * by, bz))
    columns = NRHS * (BASIS + 1)
    lower = lax.linalg.cholesky(gram[:, :columns], symmetrize_input=False)
    top, r_factor = pl.pallas_call(
        finish,
        out_shape=(
            jax.ShapeDtypeStruct((NRHS * bx * by, bz), F32),
            jax.ShapeDtypeStruct((columns, columns), F32),
        ),
        in_specs=[vmem] * 2,
        out_specs=(vmem, vmem),
        compiler_params=pltpu.CompilerParams(vmem_limit_bytes=8 << 20),
    )(top, lower)
    return top.reshape(NRHS, bx, by, bz), r_factor


def finish(top_in, lower, top, r_factor):
    top[...] = top_in[...]
    r_factor[...] = lower[...].T


def solution(mesh):
    sizes = tuple(mesh.shape[a] for a in ("gx", "gy", "gz"))
    placed = (P(None, "gx", "gy", "gz"), P("gx", "gy", "gz"), P("gx", "gy", "gz"))
    return jax.shard_map(
        functools.partial(per_device, sizes),
        mesh=mesh,
        in_specs=placed,
        out_specs=(P(None, "gx", "gy", "gz"), P()),
        check_vma=False,
    )
```
